32 devices in a mesh: chan: 16 (over z, x, core), win: 2 (over y).
Axes of the slice: x: 2, y: 2, z: 4, core: 2. Of those that a mesh axis runs over, the one named last changes fastest.
Arguments:
- records: bfloat16 [2048, 8192], P('chan', 'win')
- fir_taps: float32 [64], replicated, may hold values from -0.75 to 0.75
- pair_offsets: int32 [16, 2], P('chan'), may hold values from -4 to 5, as said below
Outputs:
- correlations: float32 [2048, 2, 33, 128], P(('chan', 'win'))
The draws below stay inside these ranges and needn't reach their ends.
Inputs may be any that keep to these rules, and one draw needn't show every extreme that they name: `pair_offsets`: each row lists one to 2 distinct offsets of -4 to 4 in its first slots and fills the remaining slots with 5, which lists no pair.
All inputs are finite; a program needn't handle non-finite values.
Results may differ from the reference program's by a relative error of at most 0.0037.
Values may be sent and summed in bfloat16 or wider, within the bound.
No kernel may reach another device: no remote copies, remote signals or barrier semaphores. Data moves between devices by JAX's collectives and lax.ppermute only.
A program may use at most 64 MiB of HBM per device.

```python
import math
import jax
import jax.numpy as jnp
from jax import lax

CH_DEV = 128
SAMPLES = 4096
TAPS = 64
DECIM = 4
MAXLAG = 16
PAIRS_MAX = 2
T_DEC = 1024
LAGS = 33
REACH = 4
CHANNELS = 2048
WINDOWS = 2
N_CHAN = 16


def draw_records(key, part):
    key_noise, key_chan, key_window = jax.random.split(jax.random.fold_in(key, 11), 3)
    chan_scale = jnp.exp(jax.random.uniform(key_chan, (CHANNELS, 1, 1), jnp.float32) * math.log(10.0))
    window_scale = jnp.exp(jax.random.uniform(key_window, (CHANNELS, WINDOWS, 1), jnp.float32) * math.log(3.0))
    noise = jax.random.normal(key_noise, (CHANNELS, WINDOWS, SAMPLES), jnp.float32)
    values = noise * chan_scale * window_scale
    return values.reshape(CHANNELS, WINDOWS * SAMPLES).astype(jnp.bfloat16)


def draw_pair_offsets(key, part):
    span = 2 * REACH + 1
    key_scores, key_row, key_counts = jax.random.split(jax.random.fold_in(key, 23), 3)
    noise = jax.random.randint(key_scores, (N_CHAN, span), 0, 1000)
    rows = jnp.arange(N_CHAN, dtype=jnp.int32)[:, None]
    columns = jnp.arange(span, dtype=jnp.int32)[None, :]
    scores = noise * span + columns
    sparse_row = jax.random.randint(key_row, (), 0, N_CHAN)
    full_row = jnp.mod(sparse_row + 1, N_CHAN)
    scores = scores + jnp.where((rows == sparse_row) & (columns == 0), 10000000, 0)
    scores = scores + jnp.where((rows == full_row) & (columns == span - 1), 10000000, 0)
    unused_values, picked = lax.top_k(scores, PAIRS_MAX)
    values = picked.astype(jnp.int32) - REACH
    counts = jax.random.randint(key_counts, (N_CHAN,), 1, PAIRS_MAX + 1)
    counts = jnp.where(rows[:, 0] == sparse_row, 1, counts)
    counts = jnp.where(rows[:, 0] == full_row, PAIRS_MAX, counts)
    slots = jnp.arange(PAIRS_MAX, dtype=jnp.int32)[None, :]
    return jnp.where(slots < counts[:, None], values, REACH + 1).astype(jnp.int32)


def scatter_about(rng, dims, deviation, limit, kind=jnp.bfloat16):
    return jnp.clip(deviation * jax.random.normal(rng, dims, jnp.float32), -limit, limit).astype(kind)


def setup_inputs(seed: int = 0) -> dict:
    key_list = jax.random.split(jax.random.key(seed), 4)
    records = draw_records(jax.random.fold_in(key_list[3], 71), 0)
    fir_taps = scatter_about(key_list[1], (TAPS,), 0.125, 0.75, jnp.float32)
    pair_offsets = draw_pair_offsets(jax.random.fold_in(key_list[3], 71), 0)
    return {"records": records, "fir_taps": fir_taps, "pair_offsets": pair_offsets}


def whiten_block(block_records, fir_taps):
    signal = block_records.astype(jnp.float32)
    signal = jnp.pad(signal, ((0, 0), (TAPS - DECIM, 0)))
    n_out = WINDOWS * T_DEC
    phases = [signal[:, phase_id::DECIM] for phase_id in range(DECIM)]
    filtered = jnp.zeros((CH_DEV, n_out), jnp.float32)
    for shift_id in range(TAPS // DECIM):
        for phase_id in range(DECIM):
            filtered = filtered + fir_taps[DECIM * shift_id + phase_id] * phases[phase_id][:, shift_id:shift_id + n_out]
    filtered = filtered.reshape(CH_DEV, WINDOWS, T_DEC)
    energy = jnp.sqrt(lax.optimization_barrier(jnp.mean(filtered * filtered, axis=2, keepdims=True)) + 1e-06)
    return (filtered / energy).astype(jnp.bfloat16)

def reference(records, fir_taps, pair_offsets):
    blocks = records.reshape(N_CHAN, CH_DEV, WINDOWS * SAMPLES)
    whitened = lax.map(lambda blk: whiten_block(blk, fir_taps), blocks)
    factor = 1.0 / math.sqrt(T_DEC * WINDOWS)

    def per_block(item):
        block_id, offset_row = item
        own_rows = lax.dynamic_index_in_dim(whitened, block_id, 0, keepdims=False).astype(jnp.float32)

        def per_slot(offset):
            other_id = jnp.mod(block_id + offset, N_CHAN).astype(jnp.int32)

            def compute(unused):
                other = lax.dynamic_index_in_dim(whitened, other_id, 0, keepdims=False).astype(jnp.float32)
                padded = jnp.pad(other, ((0, 0), (0, 0), (MAXLAG, MAXLAG)))
                stacked = jnp.stack([padded[:, :, lag_id:lag_id + T_DEC] for lag_id in range(LAGS)])
                result = jnp.einsum('iwt,ljwt->ilj', own_rows, stacked, precision=lax.Precision.HIGHEST)
                return result * factor

            def nothing(unused):
                return jnp.zeros((CH_DEV, LAGS, CH_DEV), jnp.float32)
            return lax.cond(offset <= REACH, compute, nothing, 0)
        return lax.map(per_slot, offset_row)
    block_ids = jnp.arange(N_CHAN, dtype=jnp.int32)
    result = lax.map(per_block, (block_ids, pair_offsets))
    return result.transpose(0, 2, 1, 3, 4).reshape(CHANNELS, PAIRS_MAX, LAGS, CH_DEV)
```

```python
import functools
import math

import jax
import jax.numpy as jnp
from jax import lax
from jax.experimental import pallas as pl
from jax.experimental.pallas import tpu as pltpu
from jax.sharding import PartitionSpec as P

TAPS = 64
DECIM = 4
MAXLAG = 16
T_DEC = 1024
LAGS = 33
LANES = 128
HISTORY = TAPS - DECIM
SPAN = LANES * DECIM + LANES
CHUNKS = 2
T_CHUNK = T_DEC // CHUNKS
LAG_ROWS = 32
VMEM = pltpu.VMEM
F32 = jnp.float32
BF16 = jnp.bfloat16
NT = (((1,), (1,)), ((), ()))
VMEM_SPEC = pl.BlockSpec(memory_space=pltpu.VMEM)
SMEM_SPEC = pl.BlockSpec(memory_space=pltpu.SMEM)


def shift(x, axis, by):
    n = lax.axis_size(axis)
    return lax.ppermute(x, axis, [(i, (i + by) % n) for i in range(n)])


def flip_core(x):
    n = lax.axis_size("chan")
    return lax.ppermute(x, "chan", [(i, i ^ 1) for i in range(n)])


def whiten_kernel(win, rows, tail_ref, records_ref, taps_ref, *refs):
    chunk_refs = refs[:CHUNKS]
    row_refs = refs[CHUNKS : CHUNKS + win]
    taps_scr, filtered = refs[CHUNKS + win :]
    channels = records_ref.shape[0]
    taps_scr[...] = jnp.zeros_like(taps_scr)
    taps_scr[0:1, 0:TAPS] = taps_ref[...]
    line = jnp.broadcast_to(taps_scr[0:1, :], (LANES, SPAN))
    band = pltpu.roll(line, LANES - HISTORY, 1, stride=DECIM, stride_axis=0)
    high = band.astype(BF16)
    rest = band - high.astype(F32)
    mid = rest.astype(BF16)
    low = (rest - mid.astype(F32)).astype(BF16)
    weights = jnp.concatenate([high, mid, low], axis=0)
    squares = jnp.zeros((channels, LANES), F32)
    for tile in range(T_DEC // LANES):
        start = tile * LANES * DECIM
        if tile == 0:
            raw = jnp.concatenate([tail_ref[...], records_ref[:, : SPAN - LANES]], axis=1)
        else:
            raw = records_ref[:, start - LANES : start - LANES + SPAN]
        out = lax.dot_general(raw, weights, NT, preferred_element_type=F32)
        value = out[:, :LANES] + (out[:, LANES : 2 * LANES] + out[:, 2 * LANES :])
        filtered[:, tile * LANES : (tile + 1) * LANES] = value
        squares = squares + value * value
    energy = jnp.sqrt(jnp.sum(squares, axis=1, keepdims=True) * (1.0 / T_DEC) + 1e-06)
    inverse = 1.0 / energy
    for tile in range(T_DEC // LANES):
        lanes = slice(tile * LANES, (tile + 1) * LANES)
        filtered[:, lanes] = filtered[:, lanes] * inverse
    for chunk, ref in enumerate(chunk_refs):
        ref[...] = filtered[:, chunk * T_CHUNK : (chunk + 1) * T_CHUNK].astype(BF16)
    me = lax.axis_index("win")
    for step, ref in enumerate(row_refs):
        owner = lax.rem(me + step, win)
        first = pl.multiple_of(owner * rows, rows)
        ref[...] = filtered[pl.ds(first, rows), :].astype(BF16)


def whiten(records, before, fir_taps):
    channels = records.shape[0]
    win = lax.axis_size("win")
    rows = channels // win
    return pl.pallas_call(
        functools.partial(whiten_kernel, win, rows),
        out_shape=[jax.ShapeDtypeStruct((channels, T_CHUNK), BF16)] * CHUNKS
        + [jax.ShapeDtypeStruct((rows, T_DEC), BF16)] * win,
        in_specs=[VMEM_SPEC] * 3,
        out_specs=[VMEM_SPEC] * (CHUNKS + win),
        scratch_shapes=[VMEM((8, SPAN), F32), VMEM((channels, T_DEC), F32)],
        name="whiten",
    )(before, records, fir_taps.reshape(1, TAPS))


def lags_kernel(own_ref, lags_ref, last_ref, padded):
    rows = own_ref.shape[0]
    padded[...] = jnp.zeros_like(padded)
    padded[:, LANES : LANES + T_DEC] = own_ref[...].astype(F32)
    width = T_DEC + 2 * LANES
    last_ref[...] = padded[:, LANES - MAXLAG : LANES - MAXLAG + T_DEC].astype(BF16)

    def one(i, carry):
        line = jnp.broadcast_to(padded[pl.ds(i, 1), :], (8, width))
        parts = []
        for tile in range(LAG_ROWS // 8):
            by = (8 * tile - MAXLAG) % width
            parts.append(pltpu.roll(line, by, 1, stride=1, stride_axis=0)[:, LANES : LANES + T_DEC])
        first = pl.multiple_of(i * LAG_ROWS, LAG_ROWS)
        lags_ref[pl.ds(first, LAG_ROWS), :] = jnp.concatenate(parts, axis=0).astype(BF16)
        return carry

    lax.fori_loop(0, rows, one, 0)


def lay_out_lags(own):
    rows = own.shape[0]
    return pl.pallas_call(
        lags_kernel,
        out_shape=[
            jax.ShapeDtypeStruct((rows * LAG_ROWS, T_DEC), BF16),
            jax.ShapeDtypeStruct((rows, T_DEC), BF16),
        ],
        in_specs=[VMEM_SPEC],
        out_specs=[VMEM_SPEC] * 2,
        scratch_shapes=[VMEM((rows, T_DEC + 2 * LANES), F32)],
        cost_estimate=pl.CostEstimate(flops=0, bytes_accessed=16 << 20, transcendentals=0),
        name="lags",
    )(own)


def pick_kernel(reach, own_offsets, core_offsets, *refs):
    blocks = refs[: reach + 1]
    keep_ref, send_ref = refs[reach + 1 :]
    core = lax.rem(lax.axis_index("chan"), 2)
    for offsets, lane, out_ref in ((own_offsets, core, keep_ref), (core_offsets, 1 - core, send_ref)):
        for slot in range(offsets.shape[1]):
            chip = jnp.minimum((lane + offsets[0, slot]) >> 1, reach // 2)
            for place in range(reach + 1):

                @pl.when(chip == place - reach // 2)
                def _(place=place, slot=slot, out_ref=out_ref):
                    out_ref[slot] = blocks[place][...]


def pick(reach, own_offsets, core_offsets, blocks):
    slots = own_offsets.shape[1]
    shape = jax.ShapeDtypeStruct((slots,) + blocks[0].shape, BF16)
    return pl.pallas_call(
        functools.partial(pick_kernel, reach),
        out_shape=[shape] * 2,
        in_specs=[SMEM_SPEC] * 2 + [VMEM_SPEC] * (reach + 1),
        out_specs=[VMEM_SPEC] * 2,
        name="pick",
    )(own_offsets, core_offsets, *blocks)


def merge_kernel(offsets, keep_ref, got_ref, out_ref):
    for slot in range(offsets.shape[1]):
        odd = (offsets[0, slot] & 1) == 1

        @pl.when(odd)
        def _(slot=slot):
            out_ref[slot] = got_ref[slot]

        @pl.when(jnp.logical_not(odd))
        def _(slot=slot):
            out_ref[slot] = keep_ref[slot]


def merge(offsets, keep, got):
    return pl.pallas_call(
        merge_kernel,
        out_shape=jax.ShapeDtypeStruct(keep.shape, BF16),
        in_specs=[SMEM_SPEC] + [VMEM_SPEC] * 2,
        out_specs=VMEM_SPEC,
        name="merge",
    )(offsets, keep, got)


GROUP = 8


def correlate_kernel(reach, factor, win, offsets, *refs):
    lags = refs[: 2 * win : 2]
    lasts = refs[1 : 2 * win : 2]
    others = refs[2 * win : 2 * win + win * CHUNKS]
    out_ref, stage, sems = refs[2 * win + win * CHUNKS :]
    rows = lasts[0].shape[0]
    slots = offsets.shape[1]
    steps = rows // GROUP

    def total(pick_rows):
        acc = None
        for w in range(win):
            for chunk in range(CHUNKS):
                other = others[w * CHUNKS + chunk]
                other = other[...].reshape(slots * LANES, T_CHUNK)
                part = lax.dot_general(
                    pick_rows(w, slice(chunk * T_CHUNK, (chunk + 1) * T_CHUNK)),
                    other,
                    NT,
                    preferred_element_type=F32,
                )
                acc = part if acc is None else acc + part
        return acc * factor

    last = total(lambda w, t: lasts[w][:, t])
    listed = [offsets[0, slot] <= reach for slot in range(slots)]

    def out_copy(step, place):
        first = step * GROUP
        return pltpu.make_async_copy(stage.at[place], out_ref.at[pl.ds(first, GROUP)], sems.at[place])

    for step in range(steps):
        place = step % 2
        first = step * GROUP
        acc = total(lambda w, t: lags[w][first * LAG_ROWS : (first + GROUP) * LAG_ROWS, t])
        if step >= 2:
            out_copy(step - 2, place).wait()
        for slot in range(slots):
            lanes = slice(slot * LANES, (slot + 1) * LANES)
            value = jnp.where(listed[slot], acc[:, lanes], 0.0)
            stage[place, :, slot, 0:LAG_ROWS, :] = value.reshape(GROUP, LAG_ROWS, LANES)
            tail = jnp.where(listed[slot], last[first : first + GROUP, lanes], 0.0)
            stage[place, :, slot, LAG_ROWS, :] = tail
        out_copy(step, place).start()
    for step in range(max(0, steps - 2), steps):
        out_copy(step, step % 2).wait()


def correlate(reach, factor, offsets, lags, others):
    win = len(lags)
    slots = offsets.shape[1]
    rows = lags[0][1].shape[0]
    operands = [array for pair in lags for array in pair] + others
    return pl.pallas_call(
        functools.partial(correlate_kernel, reach, factor, win),
        out_shape=jax.ShapeDtypeStruct((rows, slots, LAGS, LANES), F32),
        in_specs=[SMEM_SPEC] + [VMEM_SPEC] * len(operands),
        out_specs=pl.BlockSpec(memory_space=pl.ANY),
        scratch_shapes=[
            VMEM((2, GROUP, slots, LAGS, LANES), F32),
            pltpu.SemaphoreType.DMA((2,)),
        ],
        name="correlate",
    )(offsets, *operands)


def body(records, fir_taps, pair_offsets):
    win = lax.axis_size("win")
    reach = lax.axis_size("chan") // 4
    factor = 1.0 / math.sqrt(T_DEC * win)

    tail = records[:, records.shape[1] - LANES :]
    before = lax.ppermute(tail, "win", [(i, i + 1) for i in range(win - 1)])
    core_offsets = flip_core(pair_offsets)
    outs = whiten(records, before, fir_taps)
    chunks, row_parts = outs[:CHUNKS], outs[CHUNKS:]

    places = []
    for chunk in range(CHUNKS):
        found = {0: chunks[chunk]}
        for by in range(reach, 0, -2):
            found[-by] = shift(chunks[chunk], "chan", by)
            found[by] = shift(chunks[chunk], "chan", -by)
        places.append([found[by] for by in range(-reach, reach + 1, 2)])
    own = [row_parts[0]] + [shift(row_parts[step], "win", step) for step in range(1, win)]
    lags = [lay_out_lags(part) for part in own]

    others = [[None] * CHUNKS for _ in range(win)]
    for chunk in range(CHUNKS):
        keep, send = pick(reach, pair_offsets, core_offsets, places[chunk])
        chosen = merge(pair_offsets, keep, flip_core(send))
        others[0][chunk] = chosen
        for step in range(1, win):
            others[step][chunk] = shift(chosen, "win", step)
    flat = [array for group in others for array in group]
    return correlate(reach, factor, pair_offsets, lags, flat)


def solution(mesh):
    placed = (P("chan", "win"), P(), P("chan", None))
    return jax.shard_map(
        body,
        mesh=mesh,
        in_specs=placed,
        out_specs=P(("chan", "win"), None, None, None),
        check_vma=False,
    )
```

```python
import functools
import math

import jax
import jax.numpy as jnp
from jax import lax
from jax.experimental import pallas as pl
from jax.experimental.pallas import tpu as pltpu
from jax.sharding import PartitionSpec as P

TAPS = 64
DECIM = 4
MAXLAG = 16
T_DEC = 1024
LAGS = 33
LANES = 128
HISTORY = TAPS - DECIM
SPAN = LANES * DECIM + LANES
CHUNKS = 2
T_CHUNK = T_DEC // CHUNKS
GROUP = 16
VMEM = pltpu.VMEM
F32 = jnp.float32
BF16 = jnp.bfloat16
NT = (((1,), (1,)), ((), ()))
VMEM_SPEC = pl.BlockSpec(memory_space=pltpu.VMEM)
SMEM_SPEC = pl.BlockSpec(memory_space=pltpu.SMEM)


def shift(x, axis, by):
    n = lax.axis_size(axis)
    return lax.ppermute(x, axis, [(i, (i + by) % n) for i in range(n)])


def flip_core(x):
    n = lax.axis_size("chan")
    return lax.ppermute(x, "chan", [(i, i ^ 1) for i in range(n)])


def whiten_kernel(win, rows, tail_ref, records_ref, taps_ref, *refs):
    chunk_refs = refs[:CHUNKS]
    row_refs = refs[CHUNKS : CHUNKS + win]
    taps_scr, filtered = refs[CHUNKS + win :]
    channels = records_ref.shape[0]
    taps_scr[...] = jnp.zeros_like(taps_scr)
    taps_scr[0:1, 0:TAPS] = taps_ref[...]
    line = jnp.broadcast_to(taps_scr[0:1, :], (LANES, SPAN))
    band = pltpu.roll(line, LANES - HISTORY, 1, stride=DECIM, stride_axis=0)
    high = band.astype(BF16)
    rest = band - high.astype(F32)
    mid = rest.astype(BF16)
    low = (rest - mid.astype(F32)).astype(BF16)
    weights = jnp.concatenate([high, mid, low], axis=0)
    squares = jnp.zeros((channels, LANES), F32)
    for tile in range(T_DEC // LANES):
        start = tile * LANES * DECIM
        if tile == 0:
            raw = jnp.concatenate([tail_ref[...], records_ref[:, : SPAN - LANES]], axis=1)
        else:
            raw = records_ref[:, start - LANES : start - LANES + SPAN]
        out = lax.dot_general(raw, weights, NT, preferred_element_type=F32)
        value = out[:, :LANES] + (out[:, LANES : 2 * LANES] + out[:, 2 * LANES :])
        filtered[:, tile * LANES : (tile + 1) * LANES] = value
        squares = squares + value * value
    energy = jnp.sqrt(jnp.sum(squares, axis=1, keepdims=True) * (1.0 / T_DEC) + 1e-06)
    inverse = 1.0 / energy
    for tile in range(T_DEC // LANES):
        lanes = slice(tile * LANES, (tile + 1) * LANES)
        filtered[:, lanes] = filtered[:, lanes] * inverse
    for chunk, ref in enumerate(chunk_refs):
        ref[...] = filtered[:, chunk * T_CHUNK : (chunk + 1) * T_CHUNK].astype(BF16)
    me = lax.axis_index("win")
    for step, ref in enumerate(row_refs):
        owner = lax.rem(me + step, win)
        first = pl.multiple_of(owner * rows, rows)
        ref[...] = filtered[pl.ds(first, rows), :].astype(BF16)


def whiten(records, before, fir_taps):
    channels = records.shape[0]
    win = lax.axis_size("win")
    rows = channels // win
    return pl.pallas_call(
        functools.partial(whiten_kernel, win, rows),
        out_shape=[jax.ShapeDtypeStruct((channels, T_CHUNK), BF16)] * CHUNKS
        + [jax.ShapeDtypeStruct((rows, T_DEC), BF16)] * win,
        in_specs=[VMEM_SPEC] * 3,
        out_specs=[VMEM_SPEC] * (CHUNKS + win),
        scratch_shapes=[VMEM((8, SPAN), F32), VMEM((channels, T_DEC), F32)],
        compiler_params=pltpu.CompilerParams(vmem_limit_bytes=8 << 20),
        name="whiten",
    )(before, records, fir_taps.reshape(1, TAPS))


def lags_kernel(own_ref, lags_ref, padded):
    rows = own_ref.shape[0]
    zeros = jnp.zeros((rows, LANES), BF16)
    padded[:, :LANES] = zeros
    padded[:, LANES + T_DEC :] = zeros
    padded[:, LANES : LANES + T_DEC] = own_ref[...]
    for group in range(rows // GROUP):
        block = padded[group * GROUP : (group + 1) * GROUP, :]
        for lag in range(LAGS):
            first = LANES + MAXLAG - lag
            row = (group * LAGS + lag) * GROUP
            lags_ref[row : row + GROUP, :] = block[:, first : first + T_DEC]


def lay_out_lags(own):
    rows = own.shape[0]
    return pl.pallas_call(
        lags_kernel,
        out_shape=jax.ShapeDtypeStruct((rows * LAGS, T_DEC), BF16),
        in_specs=[VMEM_SPEC],
        out_specs=VMEM_SPEC,
        scratch_shapes=[VMEM((rows, T_DEC + 2 * LANES), BF16)],
        compiler_params=pltpu.CompilerParams(vmem_limit_bytes=8 << 20),
        cost_estimate=pl.CostEstimate(flops=0, bytes_accessed=8 << 20, transcendentals=0),
        name="lags",
    )(own)


def pick_kernel(reach, own_offsets, core_offsets, *refs):
    blocks = refs[: reach + 1]
    keep_ref, send_ref = refs[reach + 1 :]
    core = lax.rem(lax.axis_index("chan"), 2)
    for offsets, lane, out_ref in ((own_offsets, core, keep_ref), (core_offsets, 1 - core, send_ref)):
        for slot in range(offsets.shape[1]):
            chip = jnp.minimum((lane + offsets[0, slot]) >> 1, reach // 2)
            for place in range(reach + 1):

                @pl.when(chip == place - reach // 2)
                def _(place=place, slot=slot, out_ref=out_ref):
                    out_ref[slot] = blocks[place][...]


def pick(reach, own_offsets, core_offsets, blocks):
    slots = own_offsets.shape[1]
    shape = jax.ShapeDtypeStruct((slots,) + blocks[0].shape, BF16)
    return pl.pallas_call(
        functools.partial(pick_kernel, reach),
        out_shape=[shape] * 2,
        in_specs=[SMEM_SPEC] * 2 + [VMEM_SPEC] * (reach + 1),
        out_specs=[VMEM_SPEC] * 2,
        compiler_params=pltpu.CompilerParams(vmem_limit_bytes=4 << 20),
        name="pick",
    )(own_offsets, core_offsets, *blocks)


def merge_kernel(offsets, keep_ref, got_ref, out_ref):
    for slot in range(offsets.shape[1]):
        odd = (offsets[0, slot] & 1) == 1

        @pl.when(odd)
        def _(slot=slot):
            out_ref[slot] = got_ref[slot]

        @pl.when(jnp.logical_not(odd))
        def _(slot=slot):
            out_ref[slot] = keep_ref[slot]


def merge(offsets, keep, got):
    return pl.pallas_call(
        merge_kernel,
        out_shape=jax.ShapeDtypeStruct(keep.shape, BF16),
        in_specs=[SMEM_SPEC] + [VMEM_SPEC] * 2,
        out_specs=VMEM_SPEC,
        compiler_params=pltpu.CompilerParams(vmem_limit_bytes=4 << 20),
        name="merge",
    )(offsets, keep, got)


def correlate_kernel(reach, factor, win, offsets, *refs):
    lags = refs[:win]
    others = refs[win : win + win * CHUNKS]
    out_ref, stage, sems = refs[win + win * CHUNKS :]
    slots = offsets.shape[1]
    block = GROUP * LAGS
    groups = lags[0].shape[0] // block
    stride = LAGS * slots
    listed = [offsets[0, slot] <= reach for slot in range(slots)]

    def out_copy(group):
        rows = pl.ds(group * block * slots, block * slots)
        return pltpu.make_async_copy(stage.at[rows], out_ref.at[rows], sems.at[group])

    for group in range(groups):
        acc = None
        for w in range(win):
            for chunk in range(CHUNKS):
                part = lax.dot_general(
                    lags[w][group * block : (group + 1) * block, chunk * T_CHUNK : (chunk + 1) * T_CHUNK],
                    others[w * CHUNKS + chunk][...].reshape(slots * LANES, T_CHUNK),
                    NT,
                    preferred_element_type=F32,
                )
                acc = part if acc is None else acc + part
        for slot in range(slots):
            scaled = acc[:, slot * LANES : (slot + 1) * LANES] * factor
            value = jnp.where(listed[slot], scaled, 0.0)
            for lag in range(LAGS):
                for half in range(GROUP // 8):
                    row = lag * GROUP + half * 8
                    first = (group * GROUP + half * 8) * stride + lag * slots + slot
                    stage[pl.ds(first, 8, stride=stride), :] = value[row : row + 8, :]
        out_copy(group).start()
    for group in range(groups):
        out_copy(group).wait()


def correlate(reach, factor, offsets, lags, others):
    win = len(lags)
    slots = offsets.shape[1]
    total = lags[0].shape[0]
    operands = lags + others
    out = pl.pallas_call(
        functools.partial(correlate_kernel, reach, factor, win),
        out_shape=jax.ShapeDtypeStruct((total * slots, LANES), F32),
        in_specs=[SMEM_SPEC] + [VMEM_SPEC] * len(operands),
        out_specs=pl.BlockSpec(memory_space=pl.ANY),
        scratch_shapes=[
            VMEM((total * slots, LANES), F32),
            pltpu.SemaphoreType.DMA((total // (GROUP * LAGS),)),
        ],
        compiler_params=pltpu.CompilerParams(vmem_limit_bytes=24 << 20),
        name="correlate",
    )(offsets, *operands)
    return out.reshape(total // LAGS, LAGS, slots, LANES).transpose(0, 2, 1, 3)


def body(records, fir_taps, pair_offsets):
    win = lax.axis_size("win")
    reach = lax.axis_size("chan") // 4
    factor = 1.0 / math.sqrt(T_DEC * win)

    tail = records[:, records.shape[1] - LANES :]
    before = lax.ppermute(tail, "win", [(i, i + 1) for i in range(win - 1)])
    core_offsets = flip_core(pair_offsets)
    outs = whiten(records, before, fir_taps)
    chunks, row_parts = outs[:CHUNKS], outs[CHUNKS:]

    places = []
    for chunk in range(CHUNKS):
        found = {0: chunks[chunk]}
        for by in range(reach, 0, -2):
            found[-by] = shift(chunks[chunk], "chan", by)
            found[by] = shift(chunks[chunk], "chan", -by)
        places.append([found[by] for by in range(-reach, reach + 1, 2)])
    own = [row_parts[0]] + [shift(row_parts[step], "win", step) for step in range(1, win)]
    lags = [lay_out_lags(part) for part in own]

    places[0], lags[0] = lax.optimization_barrier((places[0], lags[0]))
    if CHUNKS > 1:
        places[1], lags[1:] = lax.optimization_barrier((places[1], lags[1:]))

    others = [[None] * CHUNKS for _ in range(win)]
    for chunk in range(CHUNKS):
        keep, send = pick(reach, pair_offsets, core_offsets, places[chunk])
        chosen = merge(pair_offsets, keep, flip_core(send))
        others[0][chunk] = chosen
        for step in range(1, win):
            others[step][chunk] = shift(chosen, "win", step)
    flat = [array for group in others for array in group]
    return correlate(reach, factor, pair_offsets, lags, flat)


def solution(mesh):
    placed = (P("chan", "win"), P(), P("chan", None))
    return jax.shard_map(
        body,
        mesh=mesh,
        in_specs=placed,
        out_specs=P(("chan", "win"), None, None, None),
        check_vma=False,
    )
```

```python
import functools
import math

import jax
import jax.numpy as jnp
from jax import lax
from jax.experimental import pallas as pl
from jax.experimental.pallas import tpu as pltpu
from jax.sharding import PartitionSpec as P

TAPS = 64
DECIM = 4
MAXLAG = 16
T_DEC = 1024
LAGS = 33
LANES = 128
TILES = T_DEC // LANES
HISTORY = TAPS - DECIM
RAW = LANES * DECIM
SPAN = RAW + LANES
EDGES = (0, 512, 1024)
CHUNKS = len(EDGES) - 1
TEAM = 4
GROUP = 16
VMEM = pltpu.VMEM
F32 = jnp.float32
BF16 = jnp.bfloat16
NT = (((1,), (1,)), ((), ()))
VMEM_SPEC = pl.BlockSpec(memory_space=pltpu.VMEM)
HBM_SPEC = pl.BlockSpec(memory_space=pltpu.HBM)


def grant(mib):
    return pltpu.CompilerParams(vmem_limit_bytes=mib << 20)


def shift(x, axis, by):
    n = lax.axis_size(axis)
    return lax.ppermute(x, axis, [(i, (i + by) % n) for i in range(n)])


def swap(x, bit):
    n = lax.axis_size("chan")
    return lax.ppermute(x, "chan", [(i, i ^ bit) for i in range(n)])


def filter_kernel(records_ref, taps_ref, filtered, squares_ref, band_ref, line):
    channels = filtered.shape[0]
    line[...] = jnp.zeros_like(line)
    line[0:1, 0:TAPS] = taps_ref[...]
    band = pltpu.roll(
        jnp.broadcast_to(line[0:1, :], (LANES, SPAN)), LANES - HISTORY, 1, stride=DECIM, stride_axis=0
    )
    high = band.astype(BF16)
    rest = band - high.astype(F32)
    mid = rest.astype(BF16)
    low = (rest - mid.astype(F32)).astype(BF16)
    weights = jnp.concatenate([high, mid, low], axis=0)
    band_ref[...] = weights[:, :LANES]
    squares = jnp.zeros((channels, LANES), F32)
    for tile in range(TILES):
        if tile == 0:
            block, used = records_ref[:, :RAW], weights[:, LANES:]
        else:
            block, used = records_ref[:, tile * RAW - LANES : (tile + 1) * RAW], weights
        out = lax.dot_general(block, used, NT, preferred_element_type=F32)
        value = out[:, :LANES] + (out[:, LANES : 2 * LANES] + out[:, 2 * LANES :])
        filtered[:, tile * LANES : (tile + 1) * LANES] = value
        if tile > 0:
            squares = squares + value * value
    squares_ref[...] = squares


def bulk_filter(records, fir_taps):
    channels = records.shape[0]
    return pl.pallas_call(
        filter_kernel,
        out_shape=[
            jax.ShapeDtypeStruct((channels, T_DEC), F32),
            jax.ShapeDtypeStruct((channels, LANES), F32),
            jax.ShapeDtypeStruct((3 * LANES, LANES), BF16),
        ],
        in_specs=[VMEM_SPEC] * 2,
        out_specs=[VMEM_SPEC] * 3,
        scratch_shapes=[VMEM((8, SPAN), F32)],
        compiler_params=grant(4),
        name="bulk_filter",
    )(records, fir_taps.reshape(1, TAPS))


def whiten_kernel(win, tail_ref, band_ref, filtered, squares_ref, *refs):
    chunk_refs = refs[:CHUNKS]
    row_refs = refs[CHUNKS : CHUNKS + win]
    whole_ref, white = refs[CHUNKS + win :]
    rows = row_refs[0].shape[0]
    out = lax.dot_general(tail_ref[...], band_ref[...], NT, preferred_element_type=F32)
    first = filtered[:, :LANES] + (
        out[:, :LANES] + (out[:, LANES : 2 * LANES] + out[:, 2 * LANES :])
    )
    squares = squares_ref[...] + first * first
    energy = jnp.sqrt(jnp.sum(squares, axis=1, keepdims=True) * (1.0 / T_DEC) + 1e-06)
    inverse = 1.0 / energy
    white[:, :LANES] = first * inverse
    white[:, LANES:] = filtered[:, LANES:] * inverse
    for chunk, ref in enumerate(chunk_refs):
        ref[...] = white[:, EDGES[chunk] : EDGES[chunk + 1]].astype(BF16)
    whole_ref[...] = white[...].astype(BF16)
    me = lax.axis_index("win")
    for step, ref in enumerate(row_refs):
        owner = lax.rem(me + step, win)
        ref[...] = white[pl.ds(pl.multiple_of(owner * rows, rows), rows), :].astype(BF16)


def whiten(before, band, filtered, squares):
    channels = filtered.shape[0]
    win = lax.axis_size("win")
    return pl.pallas_call(
        functools.partial(whiten_kernel, win),
        out_shape=[
            jax.ShapeDtypeStruct((channels, EDGES[chunk + 1] - EDGES[chunk]), BF16)
            for chunk in range(CHUNKS)
        ]
        + [jax.ShapeDtypeStruct((channels // win, T_DEC), BF16)] * win
        + [jax.ShapeDtypeStruct((channels, T_DEC), BF16)],
        in_specs=[VMEM_SPEC] * 4,
        out_specs=[VMEM_SPEC] * (CHUNKS + win + 1),
        scratch_shapes=[VMEM((channels, T_DEC), F32)],
        compiler_params=grant(4),
        name="whiten",
    )(before, band, filtered, squares)


def lags_kernel(own_ref, lags_ref, padded):
    rows = own_ref.shape[0]
    zeros = jnp.zeros((rows, LANES), BF16)
    padded[:, :LANES] = zeros
    padded[:, LANES + T_DEC :] = zeros
    padded[:, LANES : LANES + T_DEC] = own_ref[...]
    for group in range(rows // GROUP):
        block = padded[group * GROUP : (group + 1) * GROUP, :]
        for lag in range(LAGS):
            first = LANES + MAXLAG - lag
            row = (group * LAGS + lag) * GROUP
            lags_ref[row : row + GROUP, :] = block[:, first : first + T_DEC]


def lay_out_lags(own):
    rows = own.shape[0]
    return pl.pallas_call(
        lags_kernel,
        out_shape=jax.ShapeDtypeStruct((rows * LAGS, T_DEC), BF16),
        in_specs=[VMEM_SPEC],
        out_specs=VMEM_SPEC,
        scratch_shapes=[VMEM((rows, T_DEC + 2 * LANES), BF16)],
        compiler_params=grant(8),
        cost_estimate=pl.CostEstimate(flops=0, bytes_accessed=8 << 20, transcendentals=0),
        name="lags",
    )(own)


def far_kernel(behind_ref, ahead_ref, *refs):
    second = lax.rem(lax.axis_index("chan"), TEAM) >= 2

    @pl.when(second)
    def _():
        refs[-1][...] = behind_ref[...]

    @pl.when(jnp.logical_not(second))
    def _():
        refs[-1][...] = ahead_ref[...]


def far(behind, ahead, after):
    return pl.pallas_call(
        far_kernel,
        out_shape=jax.ShapeDtypeStruct(behind.shape, BF16),
        in_specs=[VMEM_SPEC] * (2 + len(after)),
        out_specs=VMEM_SPEC,
        compiler_params=grant(2),
        name="far",
    )(behind, ahead, *after)


def pick_kernel(hops, first, own_offsets, core_offsets, *refs):
    sources = refs[: 4 * hops + 1]
    slots = own_offsets.shape[1]
    keep_ref, send_refs = refs[-1 - slots], refs[-slots:]
    lanes = keep_ref.shape[2]
    here = lax.rem(lax.axis_index("chan"), TEAM)
    second = here >> 1
    for slot in range(slots):
        for offsets, place in ((own_offsets, here), (core_offsets, here ^ 1)):
            target = place + offsets[...][0, slot]
            hop = jnp.clip(target >> 2, -hops, hops)
            same = ((target >> 1) & 1) == second
            other = jnp.where(jnp.abs(hop) < hops, 3 * hops + hop, 4 * hops)
            index = jnp.where(same, hops + hop, other)
            for source, ref in enumerate(sources):

                @pl.when(index == source)
                def _(ref=ref, slot=slot, own=offsets is own_offsets):
                    block = ref[...] if ref.shape[1] == lanes else ref[:, first : first + lanes]
                    if own:
                        keep_ref[slot] = block
                    else:
                        send_refs[slot][...] = block


def pick(hops, first, lanes, own_offsets, core_offsets, sources, after):
    slots = own_offsets.shape[1]
    block = (sources[0].shape[0], lanes)
    out = pl.pallas_call(
        functools.partial(pick_kernel, hops, first),
        out_shape=[jax.ShapeDtypeStruct((slots,) + block, BF16)] + [jax.ShapeDtypeStruct(block, BF16)] * slots,
        in_specs=[VMEM_SPEC] * (2 + len(sources) + len(after)),
        out_specs=[VMEM_SPEC] * (1 + slots),
        compiler_params=grant(4),
        name="pick",
    )(own_offsets, core_offsets, *sources, *after)
    return out[0], out[1:]


def merge_kernel(offsets, keep_ref, *refs):
    slots = offsets.shape[1]
    odd = (offsets[...] & 1) == 1
    for slot in range(slots):
        refs[-1][slot] = jnp.where(odd[0:1, slot : slot + 1], refs[slot][...], keep_ref[slot])


def merge(offsets, keep, got, after):
    return pl.pallas_call(
        merge_kernel,
        out_shape=jax.ShapeDtypeStruct(keep.shape, BF16),
        in_specs=[VMEM_SPEC] * (2 + len(got) + len(after)),
        out_specs=VMEM_SPEC,
        compiler_params=grant(2),
        name="merge",
    )(offsets, keep, *got, *after)


def products(lags_ref, rows, parts):
    acc = None
    for first, ref in parts:
        slots, channels, lanes = ref.shape
        part = lax.dot_general(
            lags_ref[rows, first : first + lanes],
            ref[...].reshape(slots * channels, lanes),
            NT,
            preferred_element_type=F32,
        )
        acc = part if acc is None else acc + part
    return acc


def accumulate_kernel(firsts, has_acc, lags_ref, *refs):
    others = refs[: len(firsts)]
    out_ref = refs[-1]
    block = GROUP * LAGS
    for group in range(lags_ref.shape[0] // block):
        rows = slice(group * block, (group + 1) * block)
        acc = products(lags_ref, rows, list(zip(firsts, others)))
        if has_acc:
            acc = acc + refs[len(firsts)][rows, :]
        out_ref[rows, :] = acc


def accumulate(acc, lags, parts):
    firsts = [first for first, _ in parts]
    slots, channels, _ = parts[0][1].shape
    operands = [lags] + [array for _, array in parts] + ([] if acc is None else [acc])
    return pl.pallas_call(
        functools.partial(accumulate_kernel, firsts, acc is not None),
        out_shape=jax.ShapeDtypeStruct((lags.shape[0], slots * channels), F32),
        in_specs=[VMEM_SPEC] * len(operands),
        out_specs=VMEM_SPEC,
        compiler_params=grant(8),
        name="accumulate",
    )(*operands)


def finish_kernel(reach, factor, first, offsets, lags_ref, other_ref, acc_ref, out_ref, stage, sems):
    slots = offsets.shape[1]
    block = GROUP * LAGS
    stride = LAGS * slots
    groups = lags_ref.shape[0] // block
    listed = offsets[...] <= reach

    def out_copy(group):
        rows = pl.ds(group * block * slots, block * slots)
        return pltpu.make_async_copy(stage.at[rows], out_ref.at[rows], sems.at[group])

    for group in range(groups):
        rows = slice(group * block, (group + 1) * block)
        acc = (acc_ref[rows, :] + products(lags_ref, rows, [(first, other_ref)])) * factor
        for slot in range(slots):
            value = jnp.where(listed[0:1, slot : slot + 1], acc[:, slot * LANES : (slot + 1) * LANES], 0.0)
            for lag in range(LAGS):
                for half in range(GROUP // 8):
                    row = lag * GROUP + half * 8
                    start = (group * GROUP + half * 8) * stride + lag * slots + slot
                    stage[pl.ds(start, 8, stride=stride), :] = value[row : row + 8, :]
        out_copy(group).start()
    for group in range(groups):
        out_copy(group).wait()


def finish(reach, factor, offsets, acc, lags, first, other):
    slots = offsets.shape[1]
    total = lags.shape[0]
    out = pl.pallas_call(
        functools.partial(finish_kernel, reach, factor, first),
        out_shape=jax.ShapeDtypeStruct((total * slots, LANES), F32),
        in_specs=[VMEM_SPEC] * 4,
        out_specs=HBM_SPEC,
        scratch_shapes=[
            VMEM((total * slots, LANES), F32),
            pltpu.SemaphoreType.DMA((total // (GROUP * LAGS),)),
        ],
        compiler_params=grant(12),
        name="finish",
    )(offsets, lags, other, acc)
    return out.reshape(total // LAGS, LAGS, slots, LANES).transpose(0, 2, 1, 3)


def body(records, fir_taps, pair_offsets):
    win = lax.axis_size("win")
    reach = lax.axis_size("chan") // 4
    hops = reach // TEAM
    factor = 1.0 / math.sqrt(T_DEC * win)

    tail = records[:, records.shape[1] - LANES :]
    before = lax.ppermute(tail, "win", [(i, i + 1) for i in range(win - 1)])
    core_offsets = swap(pair_offsets, 1)
    filtered, squares, band = bulk_filter(records, fir_taps)
    before, core_offsets = lax.optimization_barrier((before, core_offsets))
    outs = whiten(before, band, filtered, squares)
    chunks, row_parts, whole = outs[:CHUNKS], outs[CHUNKS:-1], outs[-1]

    def spread(block):
        direct = {0: block}
        for hop in range(hops, 0, -1):
            direct[-hop] = shift(block, "chan", TEAM * hop)
            direct[hop] = shift(block, "chan", -TEAM * hop)
        return direct

    def gather(chunk, direct, after_far, after_pick, after_merge):
        edge = swap(far(direct[-hops], direct[hops], after_far), 2)
        crossed = [beside if hop == 0 else swap(direct[hop], 2) for hop in range(1 - hops, hops)]
        sources = [direct[hop] for hop in range(-hops, hops + 1)] + crossed + [edge]
        first, last = EDGES[chunk], EDGES[chunk + 1]
        keep, send = pick(hops, first, last - first, pair_offsets, core_offsets, sources, after_pick)
        chosen = merge(pair_offsets, keep, [swap(part, 1) for part in send], after_merge)
        return [chosen] + [shift(chosen, "win", step) for step in range(1, win)], send

    directs = [spread(block) for block in chunks]
    beside = swap(whole, 2)
    own = [row_parts[0]] + [shift(row_parts[step], "win", step) for step in range(1, win)]
    lags = [lay_out_lags(part) for part in own]

    pieces = []
    after_far, after_pick, after_merge = lags[:1], [], []
    for chunk in range(CHUNKS):
        piece, send = gather(chunk, directs[chunk], after_far, after_pick, after_merge)
        after_far, after_pick, after_merge = [send[0]], [piece[0]] + lags[1:], piece[1:]
        pieces.append(piece)
    others = [[pieces[chunk][step] for chunk in range(CHUNKS)] for step in range(win)]
    acc = accumulate(None, lags[0], list(zip(EDGES, others[0])))
    left = [(step, chunk) for chunk in range(CHUNKS) for step in range(1, win)]
    for step, chunk in left[:-1]:
        acc = accumulate(acc, lags[step], [(EDGES[chunk], others[step][chunk])])
    step, chunk = left[-1]
    return finish(reach, factor, pair_offsets, acc, lags[step], EDGES[chunk], others[step][chunk])


def solution(mesh):
    placed = (P("chan", "win"), P(), P("chan", None))
    return jax.shard_map(
        body,
        mesh=mesh,
        in_specs=placed,
        out_specs=P(("chan", "win"), None, None, None),
        check_vma=False,
    )
```

```python
import functools
import math

import jax
import jax.numpy as jnp
from jax import lax
from jax.experimental import pallas as pl
from jax.experimental.pallas import tpu as pltpu
from jax.sharding import PartitionSpec as P

TAPS = 64
DECIM = 4
MAXLAG = 16
T_DEC = 1024
LAGS = 33
LANES = 128
TILES = T_DEC // LANES
HISTORY = TAPS - DECIM
RAW = LANES * DECIM
SPAN = RAW + LANES
EDGES = (0, 512, 1024)
CHUNKS = len(EDGES) - 1
TEAM = 4
HEAD_GRANT = 52 << 20
GROUP = 16
VMEM = pltpu.VMEM
F32 = jnp.float32
BF16 = jnp.bfloat16
NT = (((1,), (1,)), ((), ()))
VMEM_SPEC = pl.BlockSpec(memory_space=pltpu.VMEM)
HBM_SPEC = pl.BlockSpec(memory_space=pltpu.HBM)


def grant(mib):
    return pltpu.CompilerParams(vmem_limit_bytes=mib << 20)


def shift(x, axis, by):
    n = lax.axis_size(axis)
    return lax.ppermute(x, axis, [(i, (i + by) % n) for i in range(n)])


def swap(x, bit):
    n = lax.axis_size("chan")
    return lax.ppermute(x, "chan", [(i, i ^ bit) for i in range(n)])


def head_kernel(records_ref, taps_ref, tail_out, records_out, taps_out, sems):
    last = records_ref.shape[1] - LANES
    copies = [
        pltpu.make_async_copy(taps_ref, taps_out, sems.at[0]),
        pltpu.make_async_copy(records_ref.at[:, pl.ds(last, LANES)], tail_out, sems.at[1]),
        pltpu.make_async_copy(records_ref, records_out, sems.at[2]),
    ]
    for copy in copies:
        copy.start()
    for copy in copies:
        copy.wait()


def head(records, fir_taps):
    return pl.pallas_call(
        head_kernel,
        out_shape=[
            jax.ShapeDtypeStruct((records.shape[0], LANES), BF16),
            jax.ShapeDtypeStruct(records.shape, BF16),
            jax.ShapeDtypeStruct((1, TAPS), F32),
        ],
        in_specs=[HBM_SPEC] * 2,
        out_specs=[VMEM_SPEC] * 3,
        scratch_shapes=[pltpu.SemaphoreType.DMA((3,))],
        compiler_params=pltpu.CompilerParams(vmem_limit_bytes=HEAD_GRANT),
        name="head",
    )(records, fir_taps.reshape(1, TAPS))


def filter_kernel(records_ref, taps_ref, filtered, squares_ref, band_ref, line):
    channels = filtered.shape[0]
    line[...] = jnp.zeros_like(line)
    line[0:1, 0:TAPS] = taps_ref[...]
    band = pltpu.roll(
        jnp.broadcast_to(line[0:1, :], (LANES, SPAN)), LANES - HISTORY, 1, stride=DECIM, stride_axis=0
    )
    high = band.astype(BF16)
    rest = band - high.astype(F32)
    mid = rest.astype(BF16)
    low = (rest - mid.astype(F32)).astype(BF16)
    weights = jnp.concatenate([high, mid, low], axis=0)
    band_ref[...] = weights[:, :LANES]
    blocks = [jnp.concatenate([jnp.zeros((channels, LANES), BF16), records_ref[:, :RAW]], axis=1)]
    blocks += [records_ref[:, tile * RAW - LANES : (tile + 1) * RAW] for tile in range(1, TILES)]
    out = lax.dot_general(jnp.concatenate(blocks, axis=0), weights, NT, preferred_element_type=F32)
    squares = jnp.zeros((channels, LANES), F32)
    for tile in range(TILES):
        rows = slice(tile * channels, (tile + 1) * channels)
        value = out[rows, :LANES] + (out[rows, LANES : 2 * LANES] + out[rows, 2 * LANES :])
        filtered[:, tile * LANES : (tile + 1) * LANES] = value
        if tile > 0:
            squares = squares + value * value
    squares_ref[...] = squares


def bulk_filter(records, taps):
    channels = records.shape[0]
    return pl.pallas_call(
        filter_kernel,
        out_shape=[
            jax.ShapeDtypeStruct((channels, T_DEC), F32),
            jax.ShapeDtypeStruct((channels, LANES), F32),
            jax.ShapeDtypeStruct((3 * LANES, LANES), BF16),
        ],
        in_specs=[VMEM_SPEC] * 2,
        out_specs=[VMEM_SPEC] * 3,
        scratch_shapes=[VMEM((8, SPAN), F32)],
        compiler_params=grant(4),
        name="bulk_filter",
    )(records, taps)


def whiten_kernel(win, tail_ref, band_ref, filtered, squares_ref, *refs):
    chunk_refs = refs[:CHUNKS]
    row_refs = refs[CHUNKS : CHUNKS + win]
    whole_ref, white = refs[CHUNKS + win :]
    rows = row_refs[0].shape[0]
    out = lax.dot_general(tail_ref[...], band_ref[...], NT, preferred_element_type=F32)
    first = filtered[:, :LANES] + (
        out[:, :LANES] + (out[:, LANES : 2 * LANES] + out[:, 2 * LANES :])
    )
    squares = squares_ref[...] + first * first
    energy = jnp.sqrt(jnp.sum(squares, axis=1, keepdims=True) * (1.0 / T_DEC) + 1e-06)
    inverse = 1.0 / energy
    white[:, :LANES] = first * inverse
    white[:, LANES:] = filtered[:, LANES:] * inverse
    for chunk, ref in enumerate(chunk_refs):
        ref[...] = white[:, EDGES[chunk] : EDGES[chunk + 1]].astype(BF16)
    whole_ref[...] = white[...].astype(BF16)
    me = lax.axis_index("win")
    for step, ref in enumerate(row_refs):
        owner = lax.rem(me + step, win)
        ref[...] = white[pl.ds(pl.multiple_of(owner * rows, rows), rows), :].astype(BF16)


def whiten(before, band, filtered, squares):
    channels = filtered.shape[0]
    win = lax.axis_size("win")
    return pl.pallas_call(
        functools.partial(whiten_kernel, win),
        out_shape=[
            jax.ShapeDtypeStruct((channels, EDGES[chunk + 1] - EDGES[chunk]), BF16)
            for chunk in range(CHUNKS)
        ]
        + [jax.ShapeDtypeStruct((channels // win, T_DEC), BF16)] * win
        + [jax.ShapeDtypeStruct((channels, T_DEC), BF16)],
        in_specs=[VMEM_SPEC] * 4,
        out_specs=[VMEM_SPEC] * (CHUNKS + win + 1),
        scratch_shapes=[VMEM((channels, T_DEC), F32)],
        compiler_params=grant(4),
        name="whiten",
    )(before, band, filtered, squares)


def lags_kernel(own_ref, lags_ref, padded):
    rows = own_ref.shape[0]
    zeros = jnp.zeros((rows, LANES), BF16)
    padded[:, :LANES] = zeros
    padded[:, LANES + T_DEC :] = zeros
    padded[:, LANES : LANES + T_DEC] = own_ref[...]
    for group in range(rows // GROUP):
        block = padded[group * GROUP : (group + 1) * GROUP, :]
        for lag in range(LAGS):
            first = LANES + MAXLAG - lag
            row = (group * LAGS + lag) * GROUP
            lags_ref[row : row + GROUP, :] = block[:, first : first + T_DEC]


def lay_out_lags(own):
    rows = own.shape[0]
    return pl.pallas_call(
        lags_kernel,
        out_shape=jax.ShapeDtypeStruct((rows * LAGS, T_DEC), BF16),
        in_specs=[VMEM_SPEC],
        out_specs=VMEM_SPEC,
        scratch_shapes=[VMEM((rows, T_DEC + 2 * LANES), BF16)],
        compiler_params=grant(8),
        cost_estimate=pl.CostEstimate(flops=0, bytes_accessed=8 << 20, transcendentals=0),
        name="lags",
    )(own)


def far_kernel(behind_ref, ahead_ref, *refs):
    second = lax.rem(lax.axis_index("chan"), TEAM) >= 2

    @pl.when(second)
    def _():
        refs[-1][...] = behind_ref[...]

    @pl.when(jnp.logical_not(second))
    def _():
        refs[-1][...] = ahead_ref[...]


def far(behind, ahead, after):
    return pl.pallas_call(
        far_kernel,
        out_shape=jax.ShapeDtypeStruct(behind.shape, BF16),
        in_specs=[VMEM_SPEC] * (2 + len(after)),
        out_specs=VMEM_SPEC,
        compiler_params=grant(2),
        name="far",
    )(behind, ahead, *after)


def pick_kernel(hops, first, own_offsets, core_offsets, *refs):
    sources = refs[: 4 * hops + 1]
    slots = own_offsets.shape[1]
    keep_ref, send_refs = refs[-1 - slots], refs[-slots:]
    lanes = keep_ref.shape[2]
    here = lax.rem(lax.axis_index("chan"), TEAM)
    second = here >> 1
    for slot in range(slots):
        for offsets, place in ((own_offsets, here), (core_offsets, here ^ 1)):
            target = place + offsets[...][0, slot]
            hop = jnp.clip(target >> 2, -hops, hops)
            same = ((target >> 1) & 1) == second
            other = jnp.where(jnp.abs(hop) < hops, 3 * hops + hop, 4 * hops)
            index = jnp.where(same, hops + hop, other)
            for source, ref in enumerate(sources):

                @pl.when(index == source)
                def _(ref=ref, slot=slot, own=offsets is own_offsets):
                    block = ref[...] if ref.shape[1] == lanes else ref[:, first : first + lanes]
                    if own:
                        keep_ref[slot] = block
                    else:
                        send_refs[slot][...] = block


def pick(hops, first, lanes, own_offsets, core_offsets, sources, after):
    slots = own_offsets.shape[1]
    block = (sources[0].shape[0], lanes)
    out = pl.pallas_call(
        functools.partial(pick_kernel, hops, first),
        out_shape=[jax.ShapeDtypeStruct((slots,) + block, BF16)] + [jax.ShapeDtypeStruct(block, BF16)] * slots,
        in_specs=[VMEM_SPEC] * (2 + len(sources) + len(after)),
        out_specs=[VMEM_SPEC] * (1 + slots),
        compiler_params=grant(4),
        name="pick",
    )(own_offsets, core_offsets, *sources, *after)
    return out[0], out[1:]


def merge_kernel(offsets, keep_ref, *refs):
    slots = offsets.shape[1]
    odd = (offsets[...] & 1) == 1
    for slot in range(slots):
        refs[-1][slot] = jnp.where(odd[0:1, slot : slot + 1], refs[slot][...], keep_ref[slot])


def merge(offsets, keep, got, after):
    return pl.pallas_call(
        merge_kernel,
        out_shape=jax.ShapeDtypeStruct(keep.shape, BF16),
        in_specs=[VMEM_SPEC] * (2 + len(got) + len(after)),
        out_specs=VMEM_SPEC,
        compiler_params=grant(2),
        name="merge",
    )(offsets, keep, *got, *after)


def products(lags_ref, rows, parts):
    acc = None
    for first, ref in parts:
        slots, channels, lanes = ref.shape
        part = lax.dot_general(
            lags_ref[rows, first : first + lanes],
            ref[...].reshape(slots * channels, lanes),
            NT,
            preferred_element_type=F32,
        )
        acc = part if acc is None else acc + part
    return acc


def accumulate_kernel(firsts, has_acc, lags_ref, *refs):
    others = refs[: len(firsts)]
    out_ref = refs[-1]
    block = GROUP * LAGS
    for group in range(lags_ref.shape[0] // block):
        rows = slice(group * block, (group + 1) * block)
        acc = products(lags_ref, rows, list(zip(firsts, others)))
        if has_acc:
            acc = acc + refs[len(firsts)][rows, :]
        out_ref[rows, :] = acc


def accumulate(acc, lags, parts):
    firsts = [first for first, _ in parts]
    slots, channels, _ = parts[0][1].shape
    operands = [lags] + [array for _, array in parts] + ([] if acc is None else [acc])
    return pl.pallas_call(
        functools.partial(accumulate_kernel, firsts, acc is not None),
        out_shape=jax.ShapeDtypeStruct((lags.shape[0], slots * channels), F32),
        in_specs=[VMEM_SPEC] * len(operands),
        out_specs=VMEM_SPEC,
        compiler_params=grant(8),
        name="accumulate",
    )(*operands)


def finish_kernel(reach, factor, first, offsets, lags_ref, other_ref, acc_ref, out_ref, stage, sems):
    slots = offsets.shape[1]
    block = GROUP * LAGS
    stride = LAGS * slots
    groups = lags_ref.shape[0] // block
    listed = offsets[...] <= reach

    def out_copy(group):
        rows = pl.ds(group * block * slots, block * slots)
        return pltpu.make_async_copy(stage.at[rows], out_ref.at[rows], sems.at[group])

    for group in range(groups):
        rows = slice(group * block, (group + 1) * block)
        acc = (acc_ref[rows, :] + products(lags_ref, rows, [(first, other_ref)])) * factor
        for slot in range(slots):
            value = jnp.where(listed[0:1, slot : slot + 1], acc[:, slot * LANES : (slot + 1) * LANES], 0.0)
            for lag in range(LAGS):
                for half in range(GROUP // 8):
                    row = lag * GROUP + half * 8
                    start = (group * GROUP + half * 8) * stride + lag * slots + slot
                    stage[pl.ds(start, 8, stride=stride), :] = value[row : row + 8, :]
        out_copy(group).start()
    for group in range(groups):
        out_copy(group).wait()


def finish(reach, factor, offsets, acc, lags, first, other):
    slots = offsets.shape[1]
    total = lags.shape[0]
    out = pl.pallas_call(
        functools.partial(finish_kernel, reach, factor, first),
        out_shape=jax.ShapeDtypeStruct((total * slots, LANES), F32),
        in_specs=[VMEM_SPEC] * 4,
        out_specs=HBM_SPEC,
        scratch_shapes=[
            VMEM((total * slots, LANES), F32),
            pltpu.SemaphoreType.DMA((total // (GROUP * LAGS),)),
        ],
        compiler_params=grant(12),
        name="finish",
    )(offsets, lags, other, acc)
    return out.reshape(total // LAGS, LAGS, slots, LANES).transpose(0, 2, 1, 3)


def body(records, fir_taps, pair_offsets):
    win = lax.axis_size("win")
    reach = lax.axis_size("chan") // 4
    hops = reach // TEAM
    factor = 1.0 / math.sqrt(T_DEC * win)

    tail, records, taps = head(records, fir_taps)
    before = lax.ppermute(tail, "win", [(i, i + 1) for i in range(win - 1)])
    core_offsets = swap(pair_offsets, 1)
    filtered, squares, band = bulk_filter(records, taps)
    before, core_offsets = lax.optimization_barrier((before, core_offsets))
    outs = whiten(before, band, filtered, squares)
    chunks, row_parts, whole = outs[:CHUNKS], outs[CHUNKS:-1], outs[-1]

    def spread(block):
        direct = {0: block}
        for hop in range(hops, 0, -1):
            direct[-hop] = shift(block, "chan", TEAM * hop)
            direct[hop] = shift(block, "chan", -TEAM * hop)
        return direct

    def gather(chunk, direct, after_far, after_pick, after_merge):
        edge = swap(far(direct[-hops], direct[hops], after_far), 2)
        crossed = [beside if hop == 0 else swap(direct[hop], 2) for hop in range(1 - hops, hops)]
        sources = [direct[hop] for hop in range(-hops, hops + 1)] + crossed + [edge]
        first, last = EDGES[chunk], EDGES[chunk + 1]
        keep, send = pick(hops, first, last - first, pair_offsets, core_offsets, sources, after_pick)
        chosen = merge(pair_offsets, keep, [swap(part, 1) for part in send], after_merge)
        return [chosen] + [shift(chosen, "win", step) for step in range(1, win)], send

    directs = [spread(block) for block in chunks]
    beside = swap(whole, 2)
    own = [row_parts[0]] + [shift(row_parts[step], "win", step) for step in range(1, win)]
    lags = [lay_out_lags(part) for part in own]

    pieces = []
    after_far, after_pick, after_merge = lags[:1], [], []
    for chunk in range(CHUNKS):
        piece, send = gather(chunk, directs[chunk], after_far, after_pick, after_merge)
        after_far, after_pick, after_merge = [send[0]], [piece[0]] + lags[1:], piece[1:]
        pieces.append(piece)
    others = [[pieces[chunk][step] for chunk in range(CHUNKS)] for step in range(win)]
    acc = accumulate(None, lags[0], list(zip(EDGES, others[0])))
    left = [(step, chunk) for chunk in range(CHUNKS) for step in range(1, win)]
    for step, chunk in left[:-1]:
        acc = accumulate(acc, lags[step], [(EDGES[chunk], others[step][chunk])])
    step, chunk = left[-1]
    return finish(reach, factor, pair_offsets, acc, lags[step], EDGES[chunk], others[step][chunk])


def solution(mesh):
    placed = (P("chan", "win"), P(), P("chan", None))
    return jax.shard_map(
        body,
        mesh=mesh,
        in_specs=placed,
        out_specs=P(("chan", "win"), None, None, None),
        check_vma=False,
    )
```

```python
import functools
import math

import jax
import jax.numpy as jnp
from jax import lax
from jax.experimental import pallas as pl
from jax.experimental.pallas import tpu as pltpu
from jax.sharding import PartitionSpec as P

TAPS = 64
DECIM = 4
MAXLAG = 16
T_DEC = 1024
LAGS = 33
LANES = 128
TILES = T_DEC // LANES
HISTORY = TAPS - DECIM
RAW = LANES * DECIM
SPAN = RAW + LANES
EDGES = (0, 512, 1024)
CHUNKS = len(EDGES) - 1
TEAM = 4
HEAD_GRANT = 52 << 20
GROUP = 16
VMEM = pltpu.VMEM
F32 = jnp.float32
BF16 = jnp.bfloat16
NT = (((1,), (1,)), ((), ()))
VMEM_SPEC = pl.BlockSpec(memory_space=pltpu.VMEM)
HBM_SPEC = pl.BlockSpec(memory_space=pltpu.HBM)


def grant(mib):
    return pltpu.CompilerParams(vmem_limit_bytes=mib << 20)


def shift(x, axis, by):
    n = lax.axis_size(axis)
    return lax.ppermute(x, axis, [(i, (i + by) % n) for i in range(n)])


def swap(x, bit):
    n = lax.axis_size("chan")
    return lax.ppermute(x, "chan", [(i, i ^ bit) for i in range(n)])


def head_kernel(records_ref, taps_ref, tail_out, records_out, taps_out, sems):
    last = records_ref.shape[1] - LANES
    copies = [
        pltpu.make_async_copy(taps_ref, taps_out, sems.at[0]),
        pltpu.make_async_copy(records_ref.at[:, pl.ds(last, LANES)], tail_out, sems.at[1]),
        pltpu.make_async_copy(records_ref, records_out, sems.at[2]),
    ]
    for copy in copies:
        copy.start()
    for copy in copies:
        copy.wait()


def head(records, fir_taps):
    return pl.pallas_call(
        head_kernel,
        out_shape=[
            jax.ShapeDtypeStruct((records.shape[0], LANES), BF16),
            jax.ShapeDtypeStruct(records.shape, BF16),
            jax.ShapeDtypeStruct((1, TAPS), F32),
        ],
        in_specs=[HBM_SPEC] * 2,
        out_specs=[VMEM_SPEC] * 3,
        scratch_shapes=[pltpu.SemaphoreType.DMA((3,))],
        compiler_params=pltpu.CompilerParams(vmem_limit_bytes=HEAD_GRANT),
        name="head",
    )(records, fir_taps.reshape(1, TAPS))


def filter_kernel(records_ref, taps_ref, filtered, squares_ref, band_ref, line):
    channels = filtered.shape[0]
    line[...] = jnp.zeros_like(line)
    line[0:1, 0:TAPS] = taps_ref[...]
    band = pltpu.roll(
        jnp.broadcast_to(line[0:1, :], (LANES, SPAN)), LANES - HISTORY, 1, stride=DECIM, stride_axis=0
    )
    high = band.astype(BF16)
    rest = band - high.astype(F32)
    mid = rest.astype(BF16)
    low = (rest - mid.astype(F32)).astype(BF16)
    weights = jnp.concatenate([high, mid, low], axis=0)
    band_ref[...] = weights[:, :LANES]
    blocks = [jnp.concatenate([jnp.zeros((channels, LANES), BF16), records_ref[:, :RAW]], axis=1)]
    blocks += [records_ref[:, tile * RAW - LANES : (tile + 1) * RAW] for tile in range(1, TILES)]
    out = lax.dot_general(jnp.concatenate(blocks, axis=0), weights, NT, preferred_element_type=F32)
    squares = jnp.zeros((channels, LANES), F32)
    for tile in range(TILES):
        rows = slice(tile * channels, (tile + 1) * channels)
        value = out[rows, :LANES] + (out[rows, LANES : 2 * LANES] + out[rows, 2 * LANES :])
        filtered[:, tile * LANES : (tile + 1) * LANES] = value
        if tile > 0:
            squares = squares + value * value
    squares_ref[...] = squares


def bulk_filter(records, taps):
    channels = records.shape[0]
    return pl.pallas_call(
        filter_kernel,
        out_shape=[
            jax.ShapeDtypeStruct((channels, T_DEC), F32),
            jax.ShapeDtypeStruct((channels, LANES), F32),
            jax.ShapeDtypeStruct((3 * LANES, LANES), BF16),
        ],
        in_specs=[VMEM_SPEC] * 2,
        out_specs=[VMEM_SPEC] * 3,
        scratch_shapes=[VMEM((8, SPAN), F32)],
        compiler_params=grant(4),
        name="bulk_filter",
    )(records, taps)


def whiten_kernel(win, tail_ref, band_ref, filtered, squares_ref, *refs):
    chunk_refs = refs[:CHUNKS]
    row_refs = refs[CHUNKS : CHUNKS + win]
    whole_ref, white = refs[CHUNKS + win :]
    rows = row_refs[0].shape[0]
    out = lax.dot_general(tail_ref[...], band_ref[...], NT, preferred_element_type=F32)
    first = filtered[:, :LANES] + (
        out[:, :LANES] + (out[:, LANES : 2 * LANES] + out[:, 2 * LANES :])
    )
    squares = squares_ref[...] + first * first
    energy = jnp.sqrt(jnp.sum(squares, axis=1, keepdims=True) * (1.0 / T_DEC) + 1e-06)
    inverse = 1.0 / energy
    white[:, :LANES] = first * inverse
    white[:, LANES:] = filtered[:, LANES:] * inverse
    for chunk, ref in enumerate(chunk_refs):
        ref[...] = white[:, EDGES[chunk] : EDGES[chunk + 1]].astype(BF16)
    whole_ref[...] = white[...].astype(BF16)
    me = lax.axis_index("win")
    for step, ref in enumerate(row_refs):
        owner = lax.rem(me + step, win)
        ref[...] = white[pl.ds(pl.multiple_of(owner * rows, rows), rows), :].astype(BF16)


def whiten(before, band, filtered, squares):
    channels = filtered.shape[0]
    win = lax.axis_size("win")
    return pl.pallas_call(
        functools.partial(whiten_kernel, win),
        out_shape=[
            jax.ShapeDtypeStruct((channels, EDGES[chunk + 1] - EDGES[chunk]), BF16)
            for chunk in range(CHUNKS)
        ]
        + [jax.ShapeDtypeStruct((channels // win, T_DEC), BF16)] * win
        + [jax.ShapeDtypeStruct((channels, T_DEC), BF16)],
        in_specs=[VMEM_SPEC] * 4,
        out_specs=[VMEM_SPEC] * (CHUNKS + win + 1),
        scratch_shapes=[VMEM((channels, T_DEC), F32)],
        compiler_params=grant(4),
        name="whiten",
    )(before, band, filtered, squares)


def lags_kernel(own_ref, lags_ref, padded):
    rows = own_ref.shape[0]
    zeros = jnp.zeros((rows, LANES), BF16)
    padded[:, :LANES] = zeros
    padded[:, LANES + T_DEC :] = zeros
    padded[:, LANES : LANES + T_DEC] = own_ref[...]
    for group in range(rows // GROUP):
        block = padded[group * GROUP : (group + 1) * GROUP, :]
        for lag in range(LAGS):
            first = LANES + MAXLAG - lag
            row = (group * LAGS + lag) * GROUP
            lags_ref[row : row + GROUP, :] = block[:, first : first + T_DEC]


def lay_out_lags(own):
    rows = own.shape[0]
    return pl.pallas_call(
        lags_kernel,
        out_shape=jax.ShapeDtypeStruct((rows * LAGS, T_DEC), BF16),
        in_specs=[VMEM_SPEC],
        out_specs=VMEM_SPEC,
        scratch_shapes=[VMEM((rows, T_DEC + 2 * LANES), BF16)],
        compiler_params=grant(8),
        cost_estimate=pl.CostEstimate(flops=0, bytes_accessed=8 << 20, transcendentals=0),
        name="lags",
    )(own)


def far_kernel(behind_ref, ahead_ref, *refs):
    second = lax.rem(lax.axis_index("chan"), TEAM) >= 2

    @pl.when(second)
    def _():
        refs[-1][...] = behind_ref[...]

    @pl.when(jnp.logical_not(second))
    def _():
        refs[-1][...] = ahead_ref[...]


def far(behind, ahead, after):
    return pl.pallas_call(
        far_kernel,
        out_shape=jax.ShapeDtypeStruct(behind.shape, BF16),
        in_specs=[VMEM_SPEC] * (2 + len(after)),
        out_specs=VMEM_SPEC,
        compiler_params=grant(2),
        name="far",
    )(behind, ahead, *after)


def pick_kernel(hops, first, own_offsets, core_offsets, *refs):
    sources = refs[: 4 * hops + 1]
    slots = own_offsets.shape[1]
    keep_ref, send_refs = refs[-1 - slots], refs[-slots:]
    lanes = keep_ref.shape[2]
    here = lax.rem(lax.axis_index("chan"), TEAM)
    second = here >> 1
    for slot in range(slots):
        for offsets, place in ((own_offsets, here), (core_offsets, here ^ 1)):
            target = place + offsets[...][0, slot]
            hop = jnp.clip(target >> 2, -hops, hops)
            same = ((target >> 1) & 1) == second
            other = jnp.where(jnp.abs(hop) < hops, 3 * hops + hop, 4 * hops)
            index = jnp.where(same, hops + hop, other)
            for source, ref in enumerate(sources):

                @pl.when(index == source)
                def _(ref=ref, slot=slot, own=offsets is own_offsets):
                    block = ref[...] if ref.shape[1] == lanes else ref[:, first : first + lanes]
                    if own:
                        keep_ref[slot] = block
                    else:
                        send_refs[slot][...] = block


def pick(hops, first, lanes, own_offsets, core_offsets, sources, after):
    slots = own_offsets.shape[1]
    block = (sources[0].shape[0], lanes)
    out = pl.pallas_call(
        functools.partial(pick_kernel, hops, first),
        out_shape=[jax.ShapeDtypeStruct((slots,) + block, BF16)] + [jax.ShapeDtypeStruct(block, BF16)] * slots,
        in_specs=[VMEM_SPEC] * (2 + len(sources) + len(after)),
        out_specs=[VMEM_SPEC] * (1 + slots),
        compiler_params=grant(4),
        name="pick",
    )(own_offsets, core_offsets, *sources, *after)
    return out[0], out[1:]


def merge_kernel(offsets, keep_ref, *refs):
    slots = offsets.shape[1]
    odd = (offsets[...] & 1) == 1
    for slot in range(slots):
        refs[-1][slot] = jnp.where(odd[0:1, slot : slot + 1], refs[slot][...], keep_ref[slot])


def merge(offsets, keep, got, after):
    return pl.pallas_call(
        merge_kernel,
        out_shape=jax.ShapeDtypeStruct(keep.shape, BF16),
        in_specs=[VMEM_SPEC] * (2 + len(got) + len(after)),
        out_specs=VMEM_SPEC,
        compiler_params=grant(2),
        name="merge",
    )(offsets, keep, *got, *after)


def products(lags_ref, rows, parts):
    acc = None
    for first, ref in parts:
        slots, channels, lanes = ref.shape
        part = lax.dot_general(
            lags_ref[rows, first : first + lanes],
            ref[...].reshape(slots * channels, lanes),
            NT,
            preferred_element_type=F32,
        )
        acc = part if acc is None else acc + part
    return acc


def accumulate_kernel(firsts, has_acc, lags_ref, *refs):
    others = refs[: len(firsts)]
    out_ref = refs[-1]
    block = GROUP * LAGS
    for group in range(lags_ref.shape[0] // block):
        rows = slice(group * block, (group + 1) * block)
        acc = products(lags_ref, rows, list(zip(firsts, others)))
        if has_acc:
            acc = acc + refs[len(firsts)][rows, :]
        out_ref[rows, :] = acc


def accumulate(acc, lags, parts):
    firsts = [first for first, _ in parts]
    slots, channels, _ = parts[0][1].shape
    operands = [lags] + [array for _, array in parts] + ([] if acc is None else [acc])
    return pl.pallas_call(
        functools.partial(accumulate_kernel, firsts, acc is not None),
        out_shape=jax.ShapeDtypeStruct((lags.shape[0], slots * channels), F32),
        in_specs=[VMEM_SPEC] * len(operands),
        out_specs=VMEM_SPEC,
        compiler_params=grant(8),
        name="accumulate",
    )(*operands)


def finish_kernel(reach, factor, first, offsets, lags_ref, other_ref, acc_ref, out_ref, stage, sems):
    slots = offsets.shape[1]
    block = GROUP * LAGS
    stride = LAGS * slots
    groups = lags_ref.shape[0] // block
    listed = offsets[...] <= reach

    def out_copy(group):
        rows = pl.ds(group * block * slots, block * slots)
        return pltpu.make_async_copy(stage.at[rows], out_ref.at[rows], sems.at[group])

    for group in range(groups):
        rows = slice(group * block, (group + 1) * block)
        acc = (acc_ref[rows, :] + products(lags_ref, rows, [(first, other_ref)])) * factor
        for slot in range(slots):
            value = jnp.where(listed[0:1, slot : slot + 1], acc[:, slot * LANES : (slot + 1) * LANES], 0.0)
            for lag in range(LAGS):
                for half in range(GROUP // 8):
                    row = lag * GROUP + half * 8
                    start = (group * GROUP + half * 8) * stride + lag * slots + slot
                    stage[pl.ds(start, 8, stride=stride), :] = value[row : row + 8, :]
        out_copy(group).start()
    for group in range(groups):
        out_copy(group).wait()


def finish(reach, factor, offsets, acc, lags, first, other):
    slots = offsets.shape[1]
    total = lags.shape[0]
    out = pl.pallas_call(
        functools.partial(finish_kernel, reach, factor, first),
        out_shape=jax.ShapeDtypeStruct((total * slots, LANES), F32),
        in_specs=[VMEM_SPEC] * 4,
        out_specs=HBM_SPEC,
        scratch_shapes=[
            VMEM((total * slots, LANES), F32),
            pltpu.SemaphoreType.DMA((total // (GROUP * LAGS),)),
        ],
        compiler_params=grant(12),
        name="finish",
    )(offsets, lags, other, acc)
    return out.reshape(total // LAGS, LAGS, slots, LANES).transpose(0, 2, 1, 3)


def body(records, fir_taps, pair_offsets):
    win = lax.axis_size("win")
    reach = lax.axis_size("chan") // 4
    hops = reach // TEAM
    factor = 1.0 / math.sqrt(T_DEC * win)

    tail, records, taps = head(records, fir_taps)
    before = lax.ppermute(tail, "win", [(i, i + 1) for i in range(win - 1)])
    core_offsets = swap(pair_offsets, 1)
    filtered, squares, band = bulk_filter(records, taps)
    before, core_offsets = lax.optimization_barrier((before, core_offsets))
    outs = whiten(before, band, filtered, squares)
    chunks, row_parts, whole = outs[:CHUNKS], outs[CHUNKS:-1], outs[-1]

    def spread(block):
        direct = {0: block}
        for hop in range(hops, 0, -1):
            direct[-hop] = shift(block, "chan", TEAM * hop)
            direct[hop] = shift(block, "chan", -TEAM * hop)
        return direct

    def gather(chunk, direct, after_far, after_pick, after_merge):
        edge = swap(far(direct[-hops], direct[hops], after_far), 2)
        crossed = [beside if hop == 0 else swap(direct[hop], 2) for hop in range(1 - hops, hops)]
        sources = [direct[hop] for hop in range(-hops, hops + 1)] + crossed + [edge]
        first, last = EDGES[chunk], EDGES[chunk + 1]
        keep, send = pick(hops, first, last - first, pair_offsets, core_offsets, sources, after_pick)
        chosen = merge(pair_offsets, keep, [swap(part, 1) for part in send], after_merge)
        return [chosen] + [shift(chosen, "win", step) for step in range(1, win)], send

    directs = [spread(block) for block in chunks]
    beside = swap(whole, 2)
    own = [row_parts[0]] + [shift(row_parts[step], "win", step) for step in range(1, win)]
    lags = [lay_out_lags(part) for part in own]

    pieces = []
    after_far, after_pick, after_merge = [], [], []
    for chunk in range(CHUNKS):
        piece, send = gather(chunk, directs[chunk], after_far, after_pick, after_merge)
        after_far, after_pick, after_merge = [], [piece[0]] + lags[1:], piece[1:]
        pieces.append(piece)
    others = [[pieces[chunk][step] for chunk in range(CHUNKS)] for step in range(win)]
    acc = accumulate(None, lags[0], list(zip(EDGES, others[0])))
    left = [(step, chunk) for chunk in range(CHUNKS) for step in range(1, win)]
    for step, chunk in left[:-1]:
        acc = accumulate(acc, lags[step], [(EDGES[chunk], others[step][chunk])])
    step, chunk = left[-1]
    return finish(reach, factor, pair_offsets, acc, lags[step], EDGES[chunk], others[step][chunk])


def solution(mesh):
    placed = (P("chan", "win"), P(), P("chan", None))
    return jax.shard_map(
        body,
        mesh=mesh,
        in_specs=placed,
        out_specs=P(("chan", "win"), None, None, None),
        check_vma=False,
    )
```

```python
import functools
import math

import jax
import jax.numpy as jnp
from jax import lax
from jax.experimental import pallas as pl
from jax.experimental.pallas import tpu as pltpu
from jax.sharding import PartitionSpec as P

TAPS = 64
DECIM = 4
MAXLAG = 16
T_DEC = 1024
LAGS = 33
LANES = 128
TILES = T_DEC // LANES
HISTORY = TAPS - DECIM
RAW = LANES * DECIM
SPAN = RAW + LANES
EDGES = (0, 512, 1024)
CHUNKS = len(EDGES) - 1
TEAM = 4
HEAD_GRANT = 52 << 20
GROUP = 16
VMEM = pltpu.VMEM
F32 = jnp.float32
BF16 = jnp.bfloat16
NT = (((1,), (1,)), ((), ()))
VMEM_SPEC = pl.BlockSpec(memory_space=pltpu.VMEM)
HBM_SPEC = pl.BlockSpec(memory_space=pltpu.HBM)


def grant(mib):
    return pltpu.CompilerParams(vmem_limit_bytes=mib << 20)


def shift(x, axis, by):
    n = lax.axis_size(axis)
    return lax.ppermute(x, axis, [(i, (i + by) % n) for i in range(n)])


def swap(x, bit):
    n = lax.axis_size("chan")
    return lax.ppermute(x, "chan", [(i, i ^ bit) for i in range(n)])


def head_kernel(records_ref, taps_ref, tail_out, records_out, taps_out, sems):
    last = records_ref.shape[1] - LANES
    copies = [
        pltpu.make_async_copy(taps_ref, taps_out, sems.at[0]),
        pltpu.make_async_copy(records_ref.at[:, pl.ds(last, LANES)], tail_out, sems.at[1]),
        pltpu.make_async_copy(records_ref, records_out, sems.at[2]),
    ]
    for copy in copies:
        copy.start()
    for copy in copies:
        copy.wait()


def head(records, fir_taps):
    return pl.pallas_call(
        head_kernel,
        out_shape=[
            jax.ShapeDtypeStruct((records.shape[0], LANES), BF16),
            jax.ShapeDtypeStruct(records.shape, BF16),
            jax.ShapeDtypeStruct((1, TAPS), F32),
        ],
        in_specs=[HBM_SPEC] * 2,
        out_specs=[VMEM_SPEC] * 3,
        scratch_shapes=[pltpu.SemaphoreType.DMA((3,))],
        compiler_params=pltpu.CompilerParams(vmem_limit_bytes=HEAD_GRANT),
        name="head",
    )(records, fir_taps.reshape(1, TAPS))


def filter_kernel(records_ref, taps_ref, filtered, squares_ref, band_ref, line):
    channels = filtered.shape[0]
    line[...] = jnp.zeros_like(line)
    line[0:1, 0:TAPS] = taps_ref[...]
    band = pltpu.roll(
        jnp.broadcast_to(line[0:1, :], (LANES, SPAN)), LANES - HISTORY, 1, stride=DECIM, stride_axis=0
    )
    high = band.astype(BF16)
    rest = band - high.astype(F32)
    mid = rest.astype(BF16)
    low = (rest - mid.astype(F32)).astype(BF16)
    weights = jnp.concatenate([high, mid, low], axis=0)
    band_ref[...] = weights[:, :LANES]
    blocks = [jnp.concatenate([jnp.zeros((channels, LANES), BF16), records_ref[:, :RAW]], axis=1)]
    blocks += [records_ref[:, tile * RAW - LANES : (tile + 1) * RAW] for tile in range(1, TILES)]
    out = lax.dot_general(jnp.concatenate(blocks, axis=0), weights, NT, preferred_element_type=F32)
    squares = jnp.zeros((channels, LANES), F32)
    for tile in range(TILES):
        rows = slice(tile * channels, (tile + 1) * channels)
        value = out[rows, :LANES] + (out[rows, LANES : 2 * LANES] + out[rows, 2 * LANES :])
        filtered[:, tile * LANES : (tile + 1) * LANES] = value
        if tile > 0:
            squares = squares + value * value
    squares_ref[...] = squares


def bulk_filter(records, taps):
    channels = records.shape[0]
    return pl.pallas_call(
        filter_kernel,
        out_shape=[
            jax.ShapeDtypeStruct((channels, T_DEC), F32),
            jax.ShapeDtypeStruct((channels, LANES), F32),
            jax.ShapeDtypeStruct((3 * LANES, LANES), BF16),
        ],
        in_specs=[VMEM_SPEC] * 2,
        out_specs=[VMEM_SPEC] * 3,
        scratch_shapes=[VMEM((8, SPAN), F32)],
        compiler_params=grant(4),
        name="bulk_filter",
    )(records, taps)


def whiten_kernel(win, tail_ref, band_ref, filtered, squares_ref, *refs):
    chunk_refs = refs[:CHUNKS]
    row_refs = refs[CHUNKS : CHUNKS + win]
    whole_ref, white = refs[CHUNKS + win :]
    rows = row_refs[0].shape[0]
    out = lax.dot_general(tail_ref[...], band_ref[...], NT, preferred_element_type=F32)
    first = filtered[:, :LANES] + (
        out[:, :LANES] + (out[:, LANES : 2 * LANES] + out[:, 2 * LANES :])
    )
    squares = squares_ref[...] + first * first
    energy = jnp.sqrt(jnp.sum(squares, axis=1, keepdims=True) * (1.0 / T_DEC) + 1e-06)
    inverse = 1.0 / energy
    white[:, :LANES] = first * inverse
    white[:, LANES:] = filtered[:, LANES:] * inverse
    for chunk, ref in enumerate(chunk_refs):
        ref[...] = white[:, EDGES[chunk] : EDGES[chunk + 1]].astype(BF16)
    whole_ref[...] = white[...].astype(BF16)
    me = lax.axis_index("win")
    for step, ref in enumerate(row_refs):
        owner = lax.rem(me + step, win)
        ref[...] = white[pl.ds(pl.multiple_of(owner * rows, rows), rows), :].astype(BF16)


def whiten(before, band, filtered, squares):
    channels = filtered.shape[0]
    win = lax.axis_size("win")
    return pl.pallas_call(
        functools.partial(whiten_kernel, win),
        out_shape=[
            jax.ShapeDtypeStruct((channels, EDGES[chunk + 1] - EDGES[chunk]), BF16)
            for chunk in range(CHUNKS)
        ]
        + [jax.ShapeDtypeStruct((channels // win, T_DEC), BF16)] * win
        + [jax.ShapeDtypeStruct((channels, T_DEC), BF16)],
        in_specs=[VMEM_SPEC] * 4,
        out_specs=[VMEM_SPEC] * (CHUNKS + win + 1),
        scratch_shapes=[VMEM((channels, T_DEC), F32)],
        compiler_params=grant(4),
        name="whiten",
    )(before, band, filtered, squares)


def lags_kernel(own_ref, lags_ref, padded):
    rows = own_ref.shape[0]
    zeros = jnp.zeros((rows, LANES), BF16)
    padded[:, :LANES] = zeros
    padded[:, LANES + T_DEC :] = zeros
    padded[:, LANES : LANES + T_DEC] = own_ref[...]
    for group in range(rows // GROUP):
        block = padded[group * GROUP : (group + 1) * GROUP, :]
        for lag in range(LAGS):
            first = LANES + MAXLAG - lag
            row = (group * LAGS + lag) * GROUP
            lags_ref[row : row + GROUP, :] = block[:, first : first + T_DEC]


def lay_out_lags(own):
    rows = own.shape[0]
    return pl.pallas_call(
        lags_kernel,
        out_shape=jax.ShapeDtypeStruct((rows * LAGS, T_DEC), BF16),
        in_specs=[VMEM_SPEC],
        out_specs=VMEM_SPEC,
        scratch_shapes=[VMEM((rows, T_DEC + 2 * LANES), BF16)],
        compiler_params=grant(8),
        cost_estimate=pl.CostEstimate(flops=0, bytes_accessed=8 << 20, transcendentals=0),
        name="lags",
    )(own)


def far_kernel(behind_ref, ahead_ref, *refs):
    second = lax.rem(lax.axis_index("chan"), TEAM) >= 2

    @pl.when(second)
    def _():
        refs[-1][...] = behind_ref[...]

    @pl.when(jnp.logical_not(second))
    def _():
        refs[-1][...] = ahead_ref[...]


def far(behind, ahead, after):
    return pl.pallas_call(
        far_kernel,
        out_shape=jax.ShapeDtypeStruct(behind.shape, BF16),
        in_specs=[VMEM_SPEC] * (2 + len(after)),
        out_specs=VMEM_SPEC,
        compiler_params=grant(2),
        name="far",
    )(behind, ahead, *after)


def pick_kernel(hops, first, own_offsets, core_offsets, *refs):
    sources = refs[: 4 * hops + 1]
    slots = own_offsets.shape[1]
    keep_ref, send_refs = refs[-1 - slots], refs[-slots:]
    lanes = keep_ref.shape[2]
    here = lax.rem(lax.axis_index("chan"), TEAM)
    second = here >> 1
    for slot in range(slots):
        for offsets, place in ((own_offsets, here), (core_offsets, here ^ 1)):
            target = place + offsets[...][0, slot]
            hop = jnp.clip(target >> 2, -hops, hops)
            same = ((target >> 1) & 1) == second
            other = jnp.where(jnp.abs(hop) < hops, 3 * hops + hop, 4 * hops)
            index = jnp.where(same, hops + hop, other)
            for source, ref in enumerate(sources):

                @pl.when(index == source)
                def _(ref=ref, slot=slot, own=offsets is own_offsets):
                    block = ref[...] if ref.shape[1] == lanes else ref[:, first : first + lanes]
                    if own:
                        keep_ref[slot] = block
                    else:
                        send_refs[slot][...] = block


def pick(hops, first, lanes, own_offsets, core_offsets, sources, after):
    slots = own_offsets.shape[1]
    block = (sources[0].shape[0], lanes)
    out = pl.pallas_call(
        functools.partial(pick_kernel, hops, first),
        out_shape=[jax.ShapeDtypeStruct((slots,) + block, BF16)] + [jax.ShapeDtypeStruct(block, BF16)] * slots,
        in_specs=[VMEM_SPEC] * (2 + len(sources) + len(after)),
        out_specs=[VMEM_SPEC] * (1 + slots),
        compiler_params=grant(4),
        name="pick",
    )(own_offsets, core_offsets, *sources, *after)
    return out[0], out[1:]


def merge_kernel(offsets, keep_ref, *refs):
    slots = offsets.shape[1]
    odd = (offsets[...] & 1) == 1
    for slot in range(slots):
        refs[-1][slot] = jnp.where(odd[0:1, slot : slot + 1], refs[slot][...], keep_ref[slot])


def merge(offsets, keep, got, after):
    return pl.pallas_call(
        merge_kernel,
        out_shape=jax.ShapeDtypeStruct(keep.shape, BF16),
        in_specs=[VMEM_SPEC] * (2 + len(got) + len(after)),
        out_specs=VMEM_SPEC,
        compiler_params=grant(2),
        name="merge",
    )(offsets, keep, *got, *after)


def products(lags_ref, rows, parts):
    acc = None
    for first, ref in parts:
        slots, channels, lanes = ref.shape
        part = lax.dot_general(
            lags_ref[rows, first : first + lanes],
            ref[...].reshape(slots * channels, lanes),
            NT,
            preferred_element_type=F32,
        )
        acc = part if acc is None else acc + part
    return acc


def accumulate_kernel(firsts, has_acc, lags_ref, *refs):
    others = refs[: len(firsts)]
    out_ref = refs[-1]
    block = GROUP * LAGS
    for group in range(lags_ref.shape[0] // block):
        rows = slice(group * block, (group + 1) * block)
        acc = products(lags_ref, rows, list(zip(firsts, others)))
        if has_acc:
            acc = acc + refs[len(firsts)][rows, :]
        out_ref[rows, :] = acc


def accumulate(acc, lags, parts):
    firsts = [first for first, _ in parts]
    slots, channels, _ = parts[0][1].shape
    operands = [lags] + [array for _, array in parts] + ([] if acc is None else [acc])
    return pl.pallas_call(
        functools.partial(accumulate_kernel, firsts, acc is not None),
        out_shape=jax.ShapeDtypeStruct((lags.shape[0], slots * channels), F32),
        in_specs=[VMEM_SPEC] * len(operands),
        out_specs=VMEM_SPEC,
        compiler_params=grant(8),
        name="accumulate",
    )(*operands)


def finish_kernel(reach, factor, first, offsets, lags_ref, other_ref, acc_ref, out_ref, stage, sems):
    slots = offsets.shape[1]
    block = GROUP * LAGS
    stride = LAGS * slots
    groups = lags_ref.shape[0] // block
    listed = offsets[...] <= reach

    def out_copy(group):
        rows = pl.ds(group * block * slots, block * slots)
        return pltpu.make_async_copy(stage.at[rows], out_ref.at[rows], sems.at[group])

    for group in range(groups):
        rows = slice(group * block, (group + 1) * block)
        acc = (acc_ref[rows, :] + products(lags_ref, rows, [(first, other_ref)])) * factor
        for slot in range(slots):
            value = jnp.where(listed[0:1, slot : slot + 1], acc[:, slot * LANES : (slot + 1) * LANES], 0.0)
            for lag in range(LAGS):
                for half in range(GROUP // 8):
                    row = lag * GROUP + half * 8
                    start = (group * GROUP + half * 8) * stride + lag * slots + slot
                    stage[pl.ds(start, 8, stride=stride), :] = value[row : row + 8, :]
        out_copy(group).start()
    for group in range(groups):
        out_copy(group).wait()


def finish(reach, factor, offsets, acc, lags, first, other):
    slots = offsets.shape[1]
    total = lags.shape[0]
    out = pl.pallas_call(
        functools.partial(finish_kernel, reach, factor, first),
        out_shape=jax.ShapeDtypeStruct((total * slots, LANES), F32),
        in_specs=[VMEM_SPEC] * 4,
        out_specs=HBM_SPEC,
        scratch_shapes=[
            VMEM((total * slots, LANES), F32),
            pltpu.SemaphoreType.DMA((total // (GROUP * LAGS),)),
        ],
        compiler_params=grant(12),
        name="finish",
    )(offsets, lags, other, acc)
    return out.reshape(total // LAGS, LAGS, slots, LANES).transpose(0, 2, 1, 3)


def body(records, fir_taps, pair_offsets):
    win = lax.axis_size("win")
    reach = lax.axis_size("chan") // 4
    hops = reach // TEAM
    factor = 1.0 / math.sqrt(T_DEC * win)

    tail, records, taps = head(records, fir_taps)
    before = lax.ppermute(tail, "win", [(i, i + 1) for i in range(win - 1)])
    core_offsets = swap(pair_offsets, 1)
    filtered, squares, band = bulk_filter(records, taps)
    outs = whiten(before, band, filtered, squares)
    chunks, row_parts, whole = outs[:CHUNKS], outs[CHUNKS:-1], outs[-1]

    def spread(block):
        direct = {0: block}
        for hop in range(hops, 0, -1):
            direct[-hop] = shift(block, "chan", TEAM * hop)
            direct[hop] = shift(block, "chan", -TEAM * hop)
        return direct

    def gather(chunk, direct, after_far, after_pick, after_merge):
        edge = swap(far(direct[-hops], direct[hops], after_far), 2)
        crossed = [beside if hop == 0 else swap(direct[hop], 2) for hop in range(1 - hops, hops)]
        sources = [direct[hop] for hop in range(-hops, hops + 1)] + crossed + [edge]
        first, last = EDGES[chunk], EDGES[chunk + 1]
        keep, send = pick(hops, first, last - first, pair_offsets, core_offsets, sources, after_pick)
        chosen = merge(pair_offsets, keep, [swap(part, 1) for part in send], after_merge)
        return [chosen] + [shift(chosen, "win", step) for step in range(1, win)], send

    directs = [spread(block) for block in chunks]
    beside = swap(whole, 2)
    own = [row_parts[0]] + [shift(row_parts[step], "win", step) for step in range(1, win)]
    lags = [lay_out_lags(part) for part in own]

    pieces = []
    after_far, after_pick, after_merge = [core_offsets], [], []
    for chunk in range(CHUNKS):
        piece, send = gather(chunk, directs[chunk], after_far, after_pick, after_merge)
        after_far, after_pick, after_merge = [], [piece[0]] + lags[1:], piece[1:]
        pieces.append(piece)
    others = [[pieces[chunk][step] for chunk in range(CHUNKS)] for step in range(win)]
    acc = accumulate(None, lags[0], list(zip(EDGES, others[0])))
    left = [(step, chunk) for chunk in range(CHUNKS) for step in range(1, win)]
    for step, chunk in left[:-1]:
        acc = accumulate(acc, lags[step], [(EDGES[chunk], others[step][chunk])])
    step, chunk = left[-1]
    return finish(reach, factor, pair_offsets, acc, lags[step], EDGES[chunk], others[step][chunk])


def solution(mesh):
    placed = (P("chan", "win"), P(), P("chan", None))
    return jax.shard_map(
        body,
        mesh=mesh,
        in_specs=placed,
        out_specs=P(("chan", "win"), None, None, None),
        check_vma=False,
    )
```

```python
import functools
import math

import jax
import jax.numpy as jnp
from jax import lax
from jax.experimental import pallas as pl
from jax.experimental.pallas import tpu as pltpu
from jax.sharding import PartitionSpec as P

TAPS = 64
DECIM = 4
MAXLAG = 16
T_DEC = 1024
LAGS = 33
LANES = 128
TILES = T_DEC // LANES
HISTORY = TAPS - DECIM
RAW = LANES * DECIM
SPAN = RAW + LANES
EDGES = (0, 512, 1024)
CHUNKS = len(EDGES) - 1
TEAM = 4
HEAD_GRANT = 52 << 20
GROUP = 16
VMEM = pltpu.VMEM
F32 = jnp.float32
BF16 = jnp.bfloat16
NT = (((1,), (1,)), ((), ()))
VMEM_SPEC = pl.BlockSpec(memory_space=pltpu.VMEM)
HBM_SPEC = pl.BlockSpec(memory_space=pltpu.HBM)


def grant(mib):
    return pltpu.CompilerParams(vmem_limit_bytes=mib << 20)


def shift(x, axis, by):
    n = lax.axis_size(axis)
    return lax.ppermute(x, axis, [(i, (i + by) % n) for i in range(n)])


def swap(x, bit):
    n = lax.axis_size("chan")
    return lax.ppermute(x, "chan", [(i, i ^ bit) for i in range(n)])


def head_kernel(records_ref, taps_ref, tail_out, records_out, taps_out, sems):
    last = records_ref.shape[1] - LANES
    copies = [
        pltpu.make_async_copy(taps_ref, taps_out, sems.at[0]),
        pltpu.make_async_copy(records_ref.at[:, pl.ds(last, LANES)], tail_out, sems.at[1]),
        pltpu.make_async_copy(records_ref, records_out, sems.at[2]),
    ]
    for copy in copies:
        copy.start()
    for copy in copies:
        copy.wait()


def head(records, fir_taps):
    return pl.pallas_call(
        head_kernel,
        out_shape=[
            jax.ShapeDtypeStruct((records.shape[0], LANES), BF16),
            jax.ShapeDtypeStruct(records.shape, BF16),
            jax.ShapeDtypeStruct((1, TAPS), F32),
        ],
        in_specs=[HBM_SPEC] * 2,
        out_specs=[VMEM_SPEC] * 3,
        scratch_shapes=[pltpu.SemaphoreType.DMA((3,))],
        compiler_params=pltpu.CompilerParams(vmem_limit_bytes=HEAD_GRANT),
        name="head",
    )(records, fir_taps.reshape(1, TAPS))


def filter_kernel(records_ref, taps_ref, filtered, squares_ref, band_ref, line):
    channels = filtered.shape[0]
    line[...] = jnp.zeros_like(line)
    line[0:1, 0:TAPS] = taps_ref[...]
    band = pltpu.roll(
        jnp.broadcast_to(line[0:1, :], (LANES, SPAN)), LANES - HISTORY, 1, stride=DECIM, stride_axis=0
    )
    high = band.astype(BF16)
    rest = band - high.astype(F32)
    mid = rest.astype(BF16)
    low = (rest - mid.astype(F32)).astype(BF16)
    weights = jnp.concatenate([high, mid, low], axis=0)
    band_ref[...] = weights[:, :LANES]
    blocks = [jnp.concatenate([jnp.zeros((channels, LANES), BF16), records_ref[:, :RAW]], axis=1)]
    blocks += [records_ref[:, tile * RAW - LANES : (tile + 1) * RAW] for tile in range(1, TILES)]
    out = lax.dot_general(jnp.concatenate(blocks, axis=0), weights, NT, preferred_element_type=F32)
    squares = jnp.zeros((channels, LANES), F32)
    for tile in range(TILES):
        rows = slice(tile * channels, (tile + 1) * channels)
        value = out[rows, :LANES] + (out[rows, LANES : 2 * LANES] + out[rows, 2 * LANES :])
        filtered[:, tile * LANES : (tile + 1) * LANES] = value
        if tile > 0:
            squares = squares + value * value
    squares_ref[...] = squares


def bulk_filter(records, taps):
    channels = records.shape[0]
    return pl.pallas_call(
        filter_kernel,
        out_shape=[
            jax.ShapeDtypeStruct((channels, T_DEC), F32),
            jax.ShapeDtypeStruct((channels, LANES), F32),
            jax.ShapeDtypeStruct((3 * LANES, LANES), BF16),
        ],
        in_specs=[VMEM_SPEC] * 2,
        out_specs=[VMEM_SPEC] * 3,
        scratch_shapes=[VMEM((8, SPAN), F32)],
        compiler_params=grant(4),
        name="bulk_filter",
    )(records, taps)


def whiten_kernel(win, tail_ref, band_ref, filtered, squares_ref, *refs):
    chunk_refs = refs[:CHUNKS]
    row_refs = refs[CHUNKS : CHUNKS + win]
    whole_ref, white = refs[CHUNKS + win :]
    rows = row_refs[0].shape[0]
    out = lax.dot_general(tail_ref[...], band_ref[...], NT, preferred_element_type=F32)
    first = filtered[:, :LANES] + (
        out[:, :LANES] + (out[:, LANES : 2 * LANES] + out[:, 2 * LANES :])
    )
    squares = squares_ref[...] + first * first
    energy = jnp.sqrt(jnp.sum(squares, axis=1, keepdims=True) * (1.0 / T_DEC) + 1e-06)
    inverse = 1.0 / energy
    white[:, :LANES] = first * inverse
    white[:, LANES:] = filtered[:, LANES:] * inverse
    for chunk, ref in enumerate(chunk_refs):
        ref[...] = white[:, EDGES[chunk] : EDGES[chunk + 1]].astype(BF16)
    whole_ref[...] = white[...].astype(BF16)
    me = lax.axis_index("win")
    for step, ref in enumerate(row_refs):
        owner = lax.rem(me + step, win)
        ref[...] = white[pl.ds(pl.multiple_of(owner * rows, rows), rows), :].astype(BF16)


def whiten(before, band, filtered, squares):
    channels = filtered.shape[0]
    win = lax.axis_size("win")
    return pl.pallas_call(
        functools.partial(whiten_kernel, win),
        out_shape=[
            jax.ShapeDtypeStruct((channels, EDGES[chunk + 1] - EDGES[chunk]), BF16)
            for chunk in range(CHUNKS)
        ]
        + [jax.ShapeDtypeStruct((channels // win, T_DEC), BF16)] * win
        + [jax.ShapeDtypeStruct((channels, T_DEC), BF16)],
        in_specs=[VMEM_SPEC] * 4,
        out_specs=[VMEM_SPEC] * (CHUNKS + win + 1),
        scratch_shapes=[VMEM((channels, T_DEC), F32)],
        compiler_params=grant(4),
        name="whiten",
    )(before, band, filtered, squares)


def lags_kernel(own_ref, lags_ref, padded):
    rows = own_ref.shape[0]
    zeros = jnp.zeros((rows, LANES), BF16)
    padded[:, :LANES] = zeros
    padded[:, LANES + T_DEC :] = zeros
    padded[:, LANES : LANES + T_DEC] = own_ref[...]
    for group in range(rows // GROUP):
        block = padded[group * GROUP : (group + 1) * GROUP, :]
        for lag in range(LAGS):
            first = LANES + MAXLAG - lag
            row = (group * LAGS + lag) * GROUP
            lags_ref[row : row + GROUP, :] = block[:, first : first + T_DEC]


def lay_out_lags(own):
    rows = own.shape[0]
    return pl.pallas_call(
        lags_kernel,
        out_shape=jax.ShapeDtypeStruct((rows * LAGS, T_DEC), BF16),
        in_specs=[VMEM_SPEC],
        out_specs=VMEM_SPEC,
        scratch_shapes=[VMEM((rows, T_DEC + 2 * LANES), BF16)],
        compiler_params=grant(8),
        cost_estimate=pl.CostEstimate(flops=0, bytes_accessed=8 << 20, transcendentals=0),
        name="lags",
    )(own)


def far_kernel(behind_ref, ahead_ref, *refs):
    second = lax.rem(lax.axis_index("chan"), TEAM) >= 2

    @pl.when(second)
    def _():
        refs[-1][...] = behind_ref[...]

    @pl.when(jnp.logical_not(second))
    def _():
        refs[-1][...] = ahead_ref[...]


def far(behind, ahead, after):
    return pl.pallas_call(
        far_kernel,
        out_shape=jax.ShapeDtypeStruct(behind.shape, BF16),
        in_specs=[VMEM_SPEC] * (2 + len(after)),
        out_specs=VMEM_SPEC,
        compiler_params=grant(2),
        name="far",
    )(behind, ahead, *after)


def pick_kernel(hops, first, own_offsets, core_offsets, *refs):
    sources = refs[: 4 * hops + 1]
    slots = own_offsets.shape[1]
    keep_ref, send_refs = refs[-1 - slots], refs[-slots:]
    lanes = keep_ref.shape[2]
    here = lax.rem(lax.axis_index("chan"), TEAM)
    second = here >> 1
    for slot in range(slots):
        for offsets, place in ((own_offsets, here), (core_offsets, here ^ 1)):
            target = place + offsets[...][0, slot]
            hop = jnp.clip(target >> 2, -hops, hops)
            same = ((target >> 1) & 1) == second
            other = jnp.where(jnp.abs(hop) < hops, 3 * hops + hop, 4 * hops)
            index = jnp.where(same, hops + hop, other)
            for source, ref in enumerate(sources):

                @pl.when(index == source)
                def _(ref=ref, slot=slot, own=offsets is own_offsets):
                    block = ref[...] if ref.shape[1] == lanes else ref[:, first : first + lanes]
                    if own:
                        keep_ref[slot] = block
                    else:
                        send_refs[slot][...] = block


def pick(hops, first, lanes, own_offsets, core_offsets, sources, after):
    slots = own_offsets.shape[1]
    block = (sources[0].shape[0], lanes)
    out = pl.pallas_call(
        functools.partial(pick_kernel, hops, first),
        out_shape=[jax.ShapeDtypeStruct((slots,) + block, BF16)] + [jax.ShapeDtypeStruct(block, BF16)] * slots,
        in_specs=[VMEM_SPEC] * (2 + len(sources) + len(after)),
        out_specs=[VMEM_SPEC] * (1 + slots),
        compiler_params=grant(4),
        name="pick",
    )(own_offsets, core_offsets, *sources, *after)
    return out[0], out[1:]


def merge_kernel(offsets, keep_ref, *refs):
    slots = offsets.shape[1]
    odd = (offsets[...] & 1) == 1
    for slot in range(slots):
        refs[-1][slot] = jnp.where(odd[0:1, slot : slot + 1], refs[slot][...], keep_ref[slot])


def merge(offsets, keep, got, after):
    return pl.pallas_call(
        merge_kernel,
        out_shape=jax.ShapeDtypeStruct(keep.shape, BF16),
        in_specs=[VMEM_SPEC] * (2 + len(got) + len(after)),
        out_specs=VMEM_SPEC,
        compiler_params=grant(2),
        name="merge",
    )(offsets, keep, *got, *after)


def products(lags_ref, rows, parts):
    acc = None
    for first, ref in parts:
        slots, channels, lanes = ref.shape
        part = lax.dot_general(
            lags_ref[rows, first : first + lanes],
            ref[...].reshape(slots * channels, lanes),
            NT,
            preferred_element_type=F32,
        )
        acc = part if acc is None else acc + part
    return acc


def accumulate_kernel(firsts, has_acc, lags_ref, *refs):
    others = refs[: len(firsts)]
    out_ref = refs[-1]
    block = GROUP * LAGS
    for group in range(lags_ref.shape[0] // block):
        rows = slice(group * block, (group + 1) * block)
        acc = products(lags_ref, rows, list(zip(firsts, others)))
        if has_acc:
            acc = acc + refs[len(firsts)][rows, :]
        out_ref[rows, :] = acc


def accumulate(acc, lags, parts):
    firsts = [first for first, _ in parts]
    slots, channels, _ = parts[0][1].shape
    operands = [lags] + [array for _, array in parts] + ([] if acc is None else [acc])
    return pl.pallas_call(
        functools.partial(accumulate_kernel, firsts, acc is not None),
        out_shape=jax.ShapeDtypeStruct((lags.shape[0], slots * channels), F32),
        in_specs=[VMEM_SPEC] * len(operands),
        out_specs=VMEM_SPEC,
        compiler_params=grant(8),
        name="accumulate",
    )(*operands)


def finish_kernel(reach, factor, first, offsets, lags_ref, other_ref, acc_ref, out_ref, stage, sems):
    slots = offsets.shape[1]
    block = GROUP * LAGS
    stride = LAGS * slots
    groups = lags_ref.shape[0] // block
    listed = offsets[...] <= reach

    def out_copy(group):
        rows = pl.ds(group * block * slots, block * slots)
        return pltpu.make_async_copy(stage.at[rows], out_ref.at[rows], sems.at[group])

    for group in range(groups):
        rows = slice(group * block, (group + 1) * block)
        acc = (acc_ref[rows, :] + products(lags_ref, rows, [(first, other_ref)])) * factor
        for slot in range(slots):
            value = jnp.where(listed[0:1, slot : slot + 1], acc[:, slot * LANES : (slot + 1) * LANES], 0.0)
            for lag in range(LAGS):
                for half in range(GROUP // 8):
                    row = lag * GROUP + half * 8
                    start = (group * GROUP + half * 8) * stride + lag * slots + slot
                    stage[pl.ds(start, 8, stride=stride), :] = value[row : row + 8, :]
        out_copy(group).start()
    for group in range(groups):
        out_copy(group).wait()


def finish(reach, factor, offsets, acc, lags, first, other):
    slots = offsets.shape[1]
    total = lags.shape[0]
    out = pl.pallas_call(
        functools.partial(finish_kernel, reach, factor, first),
        out_shape=jax.ShapeDtypeStruct((total * slots, LANES), F32),
        in_specs=[VMEM_SPEC] * 4,
        out_specs=HBM_SPEC,
        scratch_shapes=[
            VMEM((total * slots + 8 * LAGS * slots, LANES), F32),
            pltpu.SemaphoreType.DMA((total // (GROUP * LAGS),)),
        ],
        compiler_params=grant(12),
        name="finish",
    )(offsets, lags, other, acc)
    return out.reshape(total // LAGS, LAGS, slots, LANES).transpose(0, 2, 1, 3)


def body(records, fir_taps, pair_offsets):
    win = lax.axis_size("win")
    reach = lax.axis_size("chan") // 4
    hops = reach // TEAM
    factor = 1.0 / math.sqrt(T_DEC * win)

    tail, records, taps = head(records, fir_taps)
    before = lax.ppermute(tail, "win", [(i, i + 1) for i in range(win - 1)])
    core_offsets = swap(pair_offsets, 1)
    filtered, squares, band = bulk_filter(records, taps)
    outs = whiten(before, band, filtered, squares)
    chunks, row_parts, whole = outs[:CHUNKS], outs[CHUNKS:-1], outs[-1]

    def spread(block):
        direct = {0: block}
        for hop in range(hops, 0, -1):
            direct[-hop] = shift(block, "chan", TEAM * hop)
            direct[hop] = shift(block, "chan", -TEAM * hop)
        return direct

    def gather(chunk, direct, after_far, after_pick, after_merge):
        edge = swap(far(direct[-hops], direct[hops], after_far), 2)
        crossed = [beside if hop == 0 else swap(direct[hop], 2) for hop in range(1 - hops, hops)]
        sources = [direct[hop] for hop in range(-hops, hops + 1)] + crossed + [edge]
        first, last = EDGES[chunk], EDGES[chunk + 1]
        keep, send = pick(hops, first, last - first, pair_offsets, core_offsets, sources, after_pick)
        chosen = merge(pair_offsets, keep, [swap(part, 1) for part in send], after_merge)
        return [chosen] + [shift(chosen, "win", step) for step in range(1, win)], send

    directs = [spread(block) for block in chunks]
    beside = swap(whole, 2)
    own = [row_parts[0]] + [shift(row_parts[step], "win", step) for step in range(1, win)]
    lags = [lay_out_lags(part) for part in own]

    pieces = []
    after_far, after_pick, after_merge = [core_offsets], [], []
    for chunk in range(CHUNKS):
        piece, send = gather(chunk, directs[chunk], after_far, after_pick, after_merge)
        after_far, after_pick, after_merge = [], [piece[0]] + lags[1:], piece[1:]
        pieces.append(piece)
    others = [[pieces[chunk][step] for chunk in range(CHUNKS)] for step in range(win)]
    acc = accumulate(None, lags[0], list(zip(EDGES, others[0])))
    left = [(step, chunk) for chunk in range(CHUNKS) for step in range(1, win)]
    for step, chunk in left[:-1]:
        acc = accumulate(acc, lags[step], [(EDGES[chunk], others[step][chunk])])
    step, chunk = left[-1]
    return finish(reach, factor, pair_offsets, acc, lags[step], EDGES[chunk], others[step][chunk])


def solution(mesh):
    placed = (P("chan", "win"), P(), P("chan", None))
    return jax.shard_map(
        body,
        mesh=mesh,
        in_specs=placed,
        out_specs=P(("chan", "win"), None, None, None),
        check_vma=False,
    )
```

```python
import functools
import math

import jax
import jax.numpy as jnp
from jax import lax
from jax.experimental import pallas as pl
from jax.experimental.pallas import tpu as pltpu
from jax.sharding import PartitionSpec as P

TAPS = 64
DECIM = 4
MAXLAG = 16
T_DEC = 1024
LAGS = 33
LANES = 128
TILES = T_DEC // LANES
HISTORY = TAPS - DECIM
RAW = LANES * DECIM
SPAN = RAW + LANES
EDGES = (0, 512, 1024)
CHUNKS = len(EDGES) - 1
TEAM = 4
HEAD_GRANT = 52 << 20
BIAS = 32
GROUP = 16
VMEM = pltpu.VMEM
F32 = jnp.float32
BF16 = jnp.bfloat16
NT = (((1,), (1,)), ((), ()))
VMEM_SPEC = pl.BlockSpec(memory_space=pltpu.VMEM)
HBM_SPEC = pl.BlockSpec(memory_space=pltpu.HBM)


def grant(mib):
    return pltpu.CompilerParams(vmem_limit_bytes=mib << 20)


def shift(x, axis, by):
    n = lax.axis_size(axis)
    return lax.ppermute(x, axis, [(i, (i + by) % n) for i in range(n)])


def swap(x, bit):
    n = lax.axis_size("chan")
    return lax.ppermute(x, "chan", [(i, i ^ bit) for i in range(n)])


def head_kernel(records_ref, taps_ref, tail_out, records_out, taps_out, sems):
    last = records_ref.shape[1] - LANES
    copies = [
        pltpu.make_async_copy(taps_ref, taps_out, sems.at[0]),
        pltpu.make_async_copy(records_ref.at[:, pl.ds(last, LANES)], tail_out, sems.at[1]),
        pltpu.make_async_copy(records_ref, records_out, sems.at[2]),
    ]
    for copy in copies:
        copy.start()
    for copy in copies:
        copy.wait()


def head(records, fir_taps):
    return pl.pallas_call(
        head_kernel,
        out_shape=[
            jax.ShapeDtypeStruct((records.shape[0], LANES), BF16),
            jax.ShapeDtypeStruct(records.shape, BF16),
            jax.ShapeDtypeStruct((1, TAPS), F32),
        ],
        in_specs=[HBM_SPEC] * 2,
        out_specs=[VMEM_SPEC] * 3,
        scratch_shapes=[pltpu.SemaphoreType.DMA((3,))],
        compiler_params=pltpu.CompilerParams(vmem_limit_bytes=HEAD_GRANT),
        name="head",
    )(records, fir_taps.reshape(1, TAPS))


def filter_kernel(records_ref, taps_ref, filtered, squares_ref, band_ref, line):
    channels = filtered.shape[0]
    line[...] = jnp.zeros_like(line)
    line[0:1, 0:TAPS] = taps_ref[...]
    band = pltpu.roll(
        jnp.broadcast_to(line[0:1, :], (LANES, SPAN)), LANES - HISTORY, 1, stride=DECIM, stride_axis=0
    )
    high = band.astype(BF16)
    rest = band - high.astype(F32)
    mid = rest.astype(BF16)
    low = (rest - mid.astype(F32)).astype(BF16)
    weights = jnp.concatenate([high, mid, low], axis=0)
    band_ref[...] = weights[:, :LANES]
    blocks = [jnp.concatenate([jnp.zeros((channels, LANES), BF16), records_ref[:, :RAW]], axis=1)]
    blocks += [records_ref[:, tile * RAW - LANES : (tile + 1) * RAW] for tile in range(1, TILES)]
    out = lax.dot_general(jnp.concatenate(blocks, axis=0), weights, NT, preferred_element_type=F32)
    squares = jnp.zeros((channels, LANES), F32)
    for tile in range(TILES):
        rows = slice(tile * channels, (tile + 1) * channels)
        value = out[rows, :LANES] + (out[rows, LANES : 2 * LANES] + out[rows, 2 * LANES :])
        filtered[:, tile * LANES : (tile + 1) * LANES] = value
        if tile > 0:
            squares = squares + value * value
    squares_ref[...] = squares


def bulk_filter(records, taps):
    channels = records.shape[0]
    return pl.pallas_call(
        filter_kernel,
        out_shape=[
            jax.ShapeDtypeStruct((channels, T_DEC), F32),
            jax.ShapeDtypeStruct((channels, LANES), F32),
            jax.ShapeDtypeStruct((3 * LANES, LANES), BF16),
        ],
        in_specs=[VMEM_SPEC] * 2,
        out_specs=[VMEM_SPEC] * 3,
        scratch_shapes=[VMEM((8, SPAN), F32)],
        compiler_params=grant(4),
        name="bulk_filter",
    )(records, taps)


def whiten_kernel(win, tail_ref, band_ref, filtered, squares_ref, *refs):
    chunk_refs = refs[:CHUNKS]
    row_refs = refs[CHUNKS : CHUNKS + win]
    whole_ref, white = refs[CHUNKS + win :]
    rows = row_refs[0].shape[0]
    out = lax.dot_general(tail_ref[...], band_ref[...], NT, preferred_element_type=F32)
    first = filtered[:, :LANES] + (
        out[:, :LANES] + (out[:, LANES : 2 * LANES] + out[:, 2 * LANES :])
    )
    squares = squares_ref[...] + first * first
    energy = jnp.sqrt(jnp.sum(squares, axis=1, keepdims=True) * (1.0 / T_DEC) + 1e-06)
    inverse = 1.0 / energy
    white[:, :LANES] = first * inverse
    white[:, LANES:] = filtered[:, LANES:] * inverse
    for chunk, ref in enumerate(chunk_refs):
        ref[...] = white[:, EDGES[chunk] : EDGES[chunk + 1]].astype(BF16)
    whole_ref[...] = white[...].astype(BF16)
    me = lax.axis_index("win")
    for step, ref in enumerate(row_refs):
        owner = lax.rem(me + step, win)
        ref[...] = white[pl.ds(pl.multiple_of(owner * rows, rows), rows), :].astype(BF16)


def whiten(before, band, filtered, squares):
    channels = filtered.shape[0]
    win = lax.axis_size("win")
    return pl.pallas_call(
        functools.partial(whiten_kernel, win),
        out_shape=[
            jax.ShapeDtypeStruct((channels, EDGES[chunk + 1] - EDGES[chunk]), BF16)
            for chunk in range(CHUNKS)
        ]
        + [jax.ShapeDtypeStruct((channels // win, T_DEC), BF16)] * win
        + [jax.ShapeDtypeStruct((channels, T_DEC), BF16)],
        in_specs=[VMEM_SPEC] * 4,
        out_specs=[VMEM_SPEC] * (CHUNKS + win + 1),
        scratch_shapes=[VMEM((channels, T_DEC), F32)],
        compiler_params=grant(4),
        name="whiten",
    )(before, band, filtered, squares)


def lags_kernel(own_ref, lags_ref, padded):
    rows = own_ref.shape[0]
    zeros = jnp.zeros((rows, LANES), BF16)
    padded[:, :LANES] = zeros
    padded[:, LANES + T_DEC :] = zeros
    padded[:, LANES : LANES + T_DEC] = own_ref[...]
    for group in range(rows // GROUP):
        block = padded[group * GROUP : (group + 1) * GROUP, :]
        for lag in range(LAGS):
            first = LANES + MAXLAG - lag
            row = (group * LAGS + lag) * GROUP
            lags_ref[row : row + GROUP, :] = block[:, first : first + T_DEC]


def lay_out_lags(own):
    rows = own.shape[0]
    return pl.pallas_call(
        lags_kernel,
        out_shape=jax.ShapeDtypeStruct((rows * LAGS, T_DEC), BF16),
        in_specs=[VMEM_SPEC],
        out_specs=VMEM_SPEC,
        scratch_shapes=[VMEM((rows, T_DEC + 2 * LANES), BF16)],
        compiler_params=grant(8),
        cost_estimate=pl.CostEstimate(flops=0, bytes_accessed=8 << 20, transcendentals=0),
        name="lags",
    )(own)


def far_kernel(behind_ref, ahead_ref, *refs):
    second = lax.rem(lax.axis_index("chan"), TEAM) >= 2

    @pl.when(second)
    def _():
        refs[-1][...] = behind_ref[...]

    @pl.when(jnp.logical_not(second))
    def _():
        refs[-1][...] = ahead_ref[...]


def far(behind, ahead, after):
    return pl.pallas_call(
        far_kernel,
        out_shape=jax.ShapeDtypeStruct(behind.shape, BF16),
        in_specs=[VMEM_SPEC] * (2 + len(after)),
        out_specs=VMEM_SPEC,
        compiler_params=grant(2),
        name="far",
    )(behind, ahead, *after)


def pick_kernel(hops, first, own_offsets, core_offsets, *refs):
    sources = refs[: 4 * hops + 1]
    slots = own_offsets.shape[1]
    keep_ref, send_refs = refs[-1 - slots], refs[-slots:]
    lanes = keep_ref.shape[2]
    here = lax.rem(lax.axis_index("chan"), TEAM)
    second = here >> 1
    lane = lax.broadcasted_iota(jnp.int32, own_offsets.shape, 1)
    weight = jnp.ones(own_offsets.shape, jnp.int32)
    for slot in range(1, slots):
        weight = jnp.where(lane == slot, 1 << (6 * slot), weight)
    packed = (own_offsets[...] + BIAS) * weight + (core_offsets[...] + BIAS) * (weight << (6 * slots))
    code = jnp.sum(packed.astype(F32)).astype(jnp.int32)
    for slot in range(slots):
        for which, place in enumerate((here, here ^ 1)):
            target = place + ((code >> (6 * (slots * which + slot))) & 63) - BIAS
            hop = jnp.clip(target >> 2, -hops, hops)
            same = ((target >> 1) & 1) == second
            other = jnp.where(jnp.abs(hop) < hops, 3 * hops + hop, 4 * hops)
            index = jnp.where(same, hops + hop, other)
            for source, ref in enumerate(sources):

                @pl.when(index == source)
                def _(ref=ref, slot=slot, own=which == 0):
                    block = ref[...] if ref.shape[1] == lanes else ref[:, first : first + lanes]
                    if own:
                        keep_ref[slot] = block
                    else:
                        send_refs[slot][...] = block


def pick(hops, first, lanes, own_offsets, core_offsets, sources, after):
    slots = own_offsets.shape[1]
    block = (sources[0].shape[0], lanes)
    out = pl.pallas_call(
        functools.partial(pick_kernel, hops, first),
        out_shape=[jax.ShapeDtypeStruct((slots,) + block, BF16)] + [jax.ShapeDtypeStruct(block, BF16)] * slots,
        in_specs=[VMEM_SPEC] * (2 + len(sources) + len(after)),
        out_specs=[VMEM_SPEC] * (1 + slots),
        compiler_params=grant(4),
        name="pick",
    )(own_offsets, core_offsets, *sources, *after)
    return out[0], out[1:]


def merge_kernel(offsets, keep_ref, *refs):
    slots = offsets.shape[1]
    odd = (offsets[...] & 1) == 1
    for slot in range(slots):
        refs[-1][slot] = jnp.where(odd[0:1, slot : slot + 1], refs[slot][...], keep_ref[slot])


def merge(offsets, keep, got, after):
    return pl.pallas_call(
        merge_kernel,
        out_shape=jax.ShapeDtypeStruct(keep.shape, BF16),
        in_specs=[VMEM_SPEC] * (2 + len(got) + len(after)),
        out_specs=VMEM_SPEC,
        compiler_params=grant(2),
        name="merge",
    )(offsets, keep, *got, *after)


def products(lags_ref, rows, parts):
    acc = None
    for first, ref in parts:
        slots, channels, lanes = ref.shape
        part = lax.dot_general(
            lags_ref[rows, first : first + lanes],
            ref[...].reshape(slots * channels, lanes),
            NT,
            preferred_element_type=F32,
        )
        acc = part if acc is None else acc + part
    return acc


def accumulate_kernel(firsts, has_acc, lags_ref, *refs):
    others = refs[: len(firsts)]
    out_ref = refs[-1]
    block = GROUP * LAGS
    for group in range(lags_ref.shape[0] // block):
        rows = slice(group * block, (group + 1) * block)
        acc = products(lags_ref, rows, list(zip(firsts, others)))
        if has_acc:
            acc = acc + refs[len(firsts)][rows, :]
        out_ref[rows, :] = acc


def accumulate(acc, lags, parts):
    firsts = [first for first, _ in parts]
    slots, channels, _ = parts[0][1].shape
    operands = [lags] + [array for _, array in parts] + ([] if acc is None else [acc])
    return pl.pallas_call(
        functools.partial(accumulate_kernel, firsts, acc is not None),
        out_shape=jax.ShapeDtypeStruct((lags.shape[0], slots * channels), F32),
        in_specs=[VMEM_SPEC] * len(operands),
        out_specs=VMEM_SPEC,
        compiler_params=grant(8),
        name="accumulate",
    )(*operands)


def finish_kernel(reach, factor, first, offsets, lags_ref, other_ref, acc_ref, out_ref, stage, sems):
    slots = offsets.shape[1]
    block = GROUP * LAGS
    stride = LAGS * slots
    groups = lags_ref.shape[0] // block
    listed = offsets[...] <= reach

    def out_copy(group):
        rows = pl.ds(group * block * slots, block * slots)
        return pltpu.make_async_copy(stage.at[rows], out_ref.at[rows], sems.at[group])

    for group in range(groups):
        rows = slice(group * block, (group + 1) * block)
        acc = (acc_ref[rows, :] + products(lags_ref, rows, [(first, other_ref)])) * factor
        for slot in range(slots):
            value = jnp.where(listed[0:1, slot : slot + 1], acc[:, slot * LANES : (slot + 1) * LANES], 0.0)
            for lag in range(LAGS):
                for half in range(GROUP // 8):
                    row = lag * GROUP + half * 8
                    start = (group * GROUP + half * 8) * stride + lag * slots + slot
                    stage[pl.ds(start, 8, stride=stride), :] = value[row : row + 8, :]
        out_copy(group).start()
    for group in range(groups):
        out_copy(group).wait()


def finish(reach, factor, offsets, acc, lags, first, other):
    slots = offsets.shape[1]
    total = lags.shape[0]
    out = pl.pallas_call(
        functools.partial(finish_kernel, reach, factor, first),
        out_shape=jax.ShapeDtypeStruct((total * slots, LANES), F32),
        in_specs=[VMEM_SPEC] * 4,
        out_specs=HBM_SPEC,
        scratch_shapes=[
            VMEM((total * slots + 8 * LAGS * slots, LANES), F32),
            pltpu.SemaphoreType.DMA((total // (GROUP * LAGS),)),
        ],
        compiler_params=grant(12),
        name="finish",
    )(offsets, lags, other, acc)
    return out.reshape(total // LAGS, LAGS, slots, LANES).transpose(0, 2, 1, 3)


def body(records, fir_taps, pair_offsets):
    win = lax.axis_size("win")
    reach = lax.axis_size("chan") // 4
    hops = reach // TEAM
    factor = 1.0 / math.sqrt(T_DEC * win)

    tail, records, taps = head(records, fir_taps)
    before = lax.ppermute(tail, "win", [(i, i + 1) for i in range(win - 1)])
    core_offsets = swap(pair_offsets, 1)
    filtered, squares, band = bulk_filter(records, taps)
    outs = whiten(before, band, filtered, squares)
    chunks, row_parts, whole = outs[:CHUNKS], outs[CHUNKS:-1], outs[-1]

    def spread(block):
        direct = {0: block}
        for hop in range(hops, 0, -1):
            direct[-hop] = shift(block, "chan", TEAM * hop)
            direct[hop] = shift(block, "chan", -TEAM * hop)
        return direct

    def gather(chunk, direct, after_far, after_pick, after_merge):
        edge = swap(far(direct[-hops], direct[hops], after_far), 2)
        crossed = [beside if hop == 0 else swap(direct[hop], 2) for hop in range(1 - hops, hops)]
        sources = [direct[hop] for hop in range(-hops, hops + 1)] + crossed + [edge]
        first, last = EDGES[chunk], EDGES[chunk + 1]
        keep, send = pick(hops, first, last - first, pair_offsets, core_offsets, sources, after_pick)
        chosen = merge(pair_offsets, keep, [swap(part, 1) for part in send], after_merge)
        return [chosen] + [shift(chosen, "win", step) for step in range(1, win)], send

    directs = [spread(block) for block in chunks]
    beside = swap(whole, 2)
    own = [row_parts[0]] + [shift(row_parts[step], "win", step) for step in range(1, win)]
    lags = [lay_out_lags(part) for part in own]

    pieces = []
    after_far, after_pick, after_merge = [core_offsets] + own[1:], [], []
    for chunk in range(CHUNKS):
        piece, send = gather(chunk, directs[chunk], after_far, after_pick, after_merge)
        after_far, after_pick, after_merge = [], [piece[0]] + lags[1:], piece[1:]
        pieces.append(piece)
    others = [[pieces[chunk][step] for chunk in range(CHUNKS)] for step in range(win)]
    acc = accumulate(None, lags[0], list(zip(EDGES, others[0])))
    left = [(step, chunk) for chunk in range(CHUNKS) for step in range(1, win)]
    for step, chunk in left[:-1]:
        acc = accumulate(acc, lags[step], [(EDGES[chunk], others[step][chunk])])
    step, chunk = left[-1]
    return finish(reach, factor, pair_offsets, acc, lags[step], EDGES[chunk], others[step][chunk])


def solution(mesh):
    placed = (P("chan", "win"), P(), P("chan", None))
    return jax.shard_map(
        body,
        mesh=mesh,
        in_specs=placed,
        out_specs=P(("chan", "win"), None, None, None),
        check_vma=False,
    )
```

```python
import functools
import math

import jax
import jax.numpy as jnp
from jax import lax
from jax.experimental import pallas as pl
from jax.experimental.pallas import tpu as pltpu
from jax.sharding import PartitionSpec as P

TAPS = 64
DECIM = 4
MAXLAG = 16
T_DEC = 1024
LAGS = 33
LANES = 128
TILES = T_DEC // LANES
HISTORY = TAPS - DECIM
RAW = LANES * DECIM
SPAN = RAW + LANES
EDGES = (0, 512, 1024)
CHUNKS = len(EDGES) - 1
TEAM = 4
HEAD_GRANT = 52 << 20
GROUP = 16
VMEM = pltpu.VMEM
F32 = jnp.float32
BF16 = jnp.bfloat16
NT = (((1,), (1,)), ((), ()))
VMEM_SPEC = pl.BlockSpec(memory_space=pltpu.VMEM)
HBM_SPEC = pl.BlockSpec(memory_space=pltpu.HBM)


def grant(mib):
    return pltpu.CompilerParams(vmem_limit_bytes=mib << 20)


def shift(x, axis, by):
    n = lax.axis_size(axis)
    return lax.ppermute(x, axis, [(i, (i + by) % n) for i in range(n)])


def swap(x, bit):
    n = lax.axis_size("chan")
    return lax.ppermute(x, "chan", [(i, i ^ bit) for i in range(n)])


def head_kernel(records_ref, taps_ref, tail_out, records_out, taps_out, sems):
    last = records_ref.shape[1] - LANES
    copies = [
        pltpu.make_async_copy(taps_ref, taps_out, sems.at[0]),
        pltpu.make_async_copy(records_ref.at[:, pl.ds(last, LANES)], tail_out, sems.at[1]),
        pltpu.make_async_copy(records_ref, records_out, sems.at[2]),
    ]
    for copy in copies:
        copy.start()
    for copy in copies:
        copy.wait()


def head(records, fir_taps):
    return pl.pallas_call(
        head_kernel,
        out_shape=[
            jax.ShapeDtypeStruct((records.shape[0], LANES), BF16),
            jax.ShapeDtypeStruct(records.shape, BF16),
            jax.ShapeDtypeStruct((1, TAPS), F32),
        ],
        in_specs=[HBM_SPEC] * 2,
        out_specs=[VMEM_SPEC] * 3,
        scratch_shapes=[pltpu.SemaphoreType.DMA((3,))],
        compiler_params=pltpu.CompilerParams(vmem_limit_bytes=HEAD_GRANT),
        name="head",
    )(records, fir_taps.reshape(1, TAPS))


def filter_kernel(records_ref, taps_ref, filtered, squares_ref, band_ref, line):
    channels = filtered.shape[0]
    line[...] = jnp.zeros_like(line)
    line[0:1, 0:TAPS] = taps_ref[...]
    band = pltpu.roll(
        jnp.broadcast_to(line[0:1, :], (LANES, SPAN)), LANES - HISTORY, 1, stride=DECIM, stride_axis=0
    )
    high = band.astype(BF16)
    rest = band - high.astype(F32)
    mid = rest.astype(BF16)
    low = (rest - mid.astype(F32)).astype(BF16)
    weights = jnp.concatenate([high, mid, low], axis=0)
    band_ref[...] = weights[:, :LANES]
    blocks = [jnp.concatenate([jnp.zeros((channels, LANES), BF16), records_ref[:, :RAW]], axis=1)]
    blocks += [records_ref[:, tile * RAW - LANES : (tile + 1) * RAW] for tile in range(1, TILES)]
    out = lax.dot_general(jnp.concatenate(blocks, axis=0), weights, NT, preferred_element_type=F32)
    squares = jnp.zeros((channels, LANES), F32)
    for tile in range(TILES):
        rows = slice(tile * channels, (tile + 1) * channels)
        value = out[rows, :LANES] + (out[rows, LANES : 2 * LANES] + out[rows, 2 * LANES :])
        filtered[:, tile * LANES : (tile + 1) * LANES] = value
        if tile > 0:
            squares = squares + value * value
    squares_ref[...] = squares


def bulk_filter(records, taps):
    channels = records.shape[0]
    return pl.pallas_call(
        filter_kernel,
        out_shape=[
            jax.ShapeDtypeStruct((channels, T_DEC), F32),
            jax.ShapeDtypeStruct((channels, LANES), F32),
            jax.ShapeDtypeStruct((3 * LANES, LANES), BF16),
        ],
        in_specs=[VMEM_SPEC] * 2,
        out_specs=[VMEM_SPEC] * 3,
        scratch_shapes=[VMEM((8, SPAN), F32)],
        compiler_params=grant(4),
        name="bulk_filter",
    )(records, taps)


def whiten_kernel(win, tail_ref, band_ref, filtered, squares_ref, *refs):
    chunk_refs = refs[:CHUNKS]
    row_refs = refs[CHUNKS : CHUNKS + win]
    whole_ref, white = refs[CHUNKS + win :]
    rows = row_refs[0].shape[0]
    out = lax.dot_general(tail_ref[...], band_ref[...], NT, preferred_element_type=F32)
    first = filtered[:, :LANES] + (
        out[:, :LANES] + (out[:, LANES : 2 * LANES] + out[:, 2 * LANES :])
    )
    squares = squares_ref[...] + first * first
    energy = jnp.sqrt(jnp.sum(squares, axis=1, keepdims=True) * (1.0 / T_DEC) + 1e-06)
    inverse = 1.0 / energy
    white[:, :LANES] = first * inverse
    white[:, LANES:] = filtered[:, LANES:] * inverse
    for chunk, ref in enumerate(chunk_refs):
        ref[...] = white[:, EDGES[chunk] : EDGES[chunk + 1]].astype(BF16)
    whole_ref[...] = white[...].astype(BF16)
    me = lax.axis_index("win")
    for step, ref in enumerate(row_refs):
        owner = lax.rem(me + step, win)
        ref[...] = white[pl.ds(pl.multiple_of(owner * rows, rows), rows), :].astype(BF16)


def whiten(before, band, filtered, squares):
    channels = filtered.shape[0]
    win = lax.axis_size("win")
    return pl.pallas_call(
        functools.partial(whiten_kernel, win),
        out_shape=[
            jax.ShapeDtypeStruct((channels, EDGES[chunk + 1] - EDGES[chunk]), BF16)
            for chunk in range(CHUNKS)
        ]
        + [jax.ShapeDtypeStruct((channels // win, T_DEC), BF16)] * win
        + [jax.ShapeDtypeStruct((channels, T_DEC), BF16)],
        in_specs=[VMEM_SPEC] * 4,
        out_specs=[VMEM_SPEC] * (CHUNKS + win + 1),
        scratch_shapes=[VMEM((channels, T_DEC), F32)],
        compiler_params=grant(4),
        name="whiten",
    )(before, band, filtered, squares)


def lags_kernel(own_ref, lags_ref, padded):
    rows = own_ref.shape[0]
    zeros = jnp.zeros((rows, LANES), BF16)
    padded[:, :LANES] = zeros
    padded[:, LANES + T_DEC :] = zeros
    padded[:, LANES : LANES + T_DEC] = own_ref[...]
    for group in range(rows // GROUP):
        block = padded[group * GROUP : (group + 1) * GROUP, :]
        for lag in range(LAGS):
            first = LANES + MAXLAG - lag
            row = (group * LAGS + lag) * GROUP
            lags_ref[row : row + GROUP, :] = block[:, first : first + T_DEC]


def lay_out_lags(own):
    rows = own.shape[0]
    return pl.pallas_call(
        lags_kernel,
        out_shape=jax.ShapeDtypeStruct((rows * LAGS, T_DEC), BF16),
        in_specs=[VMEM_SPEC],
        out_specs=VMEM_SPEC,
        scratch_shapes=[VMEM((rows, T_DEC + 2 * LANES), BF16)],
        compiler_params=grant(8),
        cost_estimate=pl.CostEstimate(flops=0, bytes_accessed=8 << 20, transcendentals=0),
        name="lags",
    )(own)


def far_kernel(behind_ref, ahead_ref, *refs):
    second = lax.rem(lax.axis_index("chan"), TEAM) >= 2

    @pl.when(second)
    def _():
        refs[-1][...] = behind_ref[...]

    @pl.when(jnp.logical_not(second))
    def _():
        refs[-1][...] = ahead_ref[...]


def far(behind, ahead, after):
    return pl.pallas_call(
        far_kernel,
        out_shape=jax.ShapeDtypeStruct(behind.shape, BF16),
        in_specs=[VMEM_SPEC] * (2 + len(after)),
        out_specs=VMEM_SPEC,
        compiler_params=grant(2),
        name="far",
    )(behind, ahead, *after)


def pick_kernel(hops, first, own_offsets, core_offsets, *refs):
    sources = refs[: 4 * hops + 1]
    slots = own_offsets.shape[1]
    keep_ref, send_refs = refs[-1 - slots], refs[-slots:]
    lanes = keep_ref.shape[2]
    here = lax.rem(lax.axis_index("chan"), TEAM)
    second = here >> 1
    for slot in range(slots):
        for offsets, place in ((own_offsets, here), (core_offsets, here ^ 1)):
            target = place + offsets[...][0, slot]
            hop = jnp.clip(target >> 2, -hops, hops)
            same = ((target >> 1) & 1) == second
            other = jnp.where(jnp.abs(hop) < hops, 3 * hops + hop, 4 * hops)
            index = jnp.where(same, hops + hop, other)
            for source, ref in enumerate(sources):

                @pl.when(index == source)
                def _(ref=ref, slot=slot, own=offsets is own_offsets):
                    block = ref[...] if ref.shape[1] == lanes else ref[:, first : first + lanes]
                    if own:
                        keep_ref[slot] = block
                    else:
                        send_refs[slot][...] = block


def pick(hops, first, lanes, own_offsets, core_offsets, sources, after):
    slots = own_offsets.shape[1]
    block = (sources[0].shape[0], lanes)
    out = pl.pallas_call(
        functools.partial(pick_kernel, hops, first),
        out_shape=[jax.ShapeDtypeStruct((slots,) + block, BF16)] + [jax.ShapeDtypeStruct(block, BF16)] * slots,
        in_specs=[VMEM_SPEC] * (2 + len(sources) + len(after)),
        out_specs=[VMEM_SPEC] * (1 + slots),
        compiler_params=grant(4),
        name="pick",
    )(own_offsets, core_offsets, *sources, *after)
    return out[0], out[1:]


def merge_kernel(offsets, keep_ref, *refs):
    slots = offsets.shape[1]
    odd = (offsets[...] & 1) == 1
    for slot in range(slots):
        refs[-1][slot] = jnp.where(odd[0:1, slot : slot + 1], refs[slot][...], keep_ref[slot])


def merge(offsets, keep, got, after):
    return pl.pallas_call(
        merge_kernel,
        out_shape=jax.ShapeDtypeStruct(keep.shape, BF16),
        in_specs=[VMEM_SPEC] * (2 + len(got) + len(after)),
        out_specs=VMEM_SPEC,
        compiler_params=grant(2),
        name="merge",
    )(offsets, keep, *got, *after)


def products(lags_ref, rows, parts):
    acc = None
    for first, ref in parts:
        slots, channels, lanes = ref.shape
        part = lax.dot_general(
            lags_ref[rows, first : first + lanes],
            ref[...].reshape(slots * channels, lanes),
            NT,
            preferred_element_type=F32,
        )
        acc = part if acc is None else acc + part
    return acc


def accumulate_kernel(firsts, has_acc, lags_ref, *refs):
    others = refs[: len(firsts)]
    out_ref = refs[-1]
    block = GROUP * LAGS
    for group in range(lags_ref.shape[0] // block):
        rows = slice(group * block, (group + 1) * block)
        acc = products(lags_ref, rows, list(zip(firsts, others)))
        if has_acc:
            acc = acc + refs[len(firsts)][rows, :]
        out_ref[rows, :] = acc


def accumulate(acc, lags, parts):
    firsts = [first for first, _ in parts]
    slots, channels, _ = parts[0][1].shape
    operands = [lags] + [array for _, array in parts] + ([] if acc is None else [acc])
    return pl.pallas_call(
        functools.partial(accumulate_kernel, firsts, acc is not None),
        out_shape=jax.ShapeDtypeStruct((lags.shape[0], slots * channels), F32),
        in_specs=[VMEM_SPEC] * len(operands),
        out_specs=VMEM_SPEC,
        compiler_params=grant(8),
        name="accumulate",
    )(*operands)


def finish_kernel(reach, factor, first, offsets, lags_ref, other_ref, acc_ref, out_ref, stage, sems):
    slots = offsets.shape[1]
    block = GROUP * LAGS
    stride = LAGS * slots
    groups = lags_ref.shape[0] // block
    listed = offsets[...] <= reach

    def out_copy(group):
        rows = pl.ds(group * block * slots, block * slots)
        return pltpu.make_async_copy(stage.at[rows], out_ref.at[rows], sems.at[group])

    for group in range(groups):
        rows = slice(group * block, (group + 1) * block)
        acc = (acc_ref[rows, :] + products(lags_ref, rows, [(first, other_ref)])) * factor
        for slot in range(slots):
            value = jnp.where(listed[0:1, slot : slot + 1], acc[:, slot * LANES : (slot + 1) * LANES], 0.0)
            for lag in range(LAGS):
                for half in range(GROUP // 8):
                    row = lag * GROUP + half * 8
                    start = (group * GROUP + half * 8) * stride + lag * slots + slot
                    stage[pl.ds(start, 8, stride=stride), :] = value[row : row + 8, :]
        out_copy(group).start()
    for group in range(groups):
        out_copy(group).wait()


def finish(reach, factor, offsets, acc, lags, first, other):
    slots = offsets.shape[1]
    total = lags.shape[0]
    out = pl.pallas_call(
        functools.partial(finish_kernel, reach, factor, first),
        out_shape=jax.ShapeDtypeStruct((total * slots, LANES), F32),
        in_specs=[VMEM_SPEC] * 4,
        out_specs=HBM_SPEC,
        scratch_shapes=[
            VMEM((total * slots + 8 * LAGS * slots, LANES), F32),
            pltpu.SemaphoreType.DMA((total // (GROUP * LAGS),)),
        ],
        compiler_params=grant(12),
        name="finish",
    )(offsets, lags, other, acc)
    return out.reshape(total // LAGS, LAGS, slots, LANES).transpose(0, 2, 1, 3)


def body(records, fir_taps, pair_offsets):
    win = lax.axis_size("win")
    reach = lax.axis_size("chan") // 4
    hops = reach // TEAM
    factor = 1.0 / math.sqrt(T_DEC * win)

    tail, records, taps = head(records, fir_taps)
    before = lax.ppermute(tail, "win", [(i, i + 1) for i in range(win - 1)])
    core_offsets = swap(pair_offsets, 1)
    filtered, squares, band = bulk_filter(records, taps)
    outs = whiten(before, band, filtered, squares)
    chunks, row_parts, whole = outs[:CHUNKS], outs[CHUNKS:-1], outs[-1]

    def spread(block):
        direct = {0: block}
        for hop in range(hops, 0, -1):
            direct[-hop] = shift(block, "chan", TEAM * hop)
            direct[hop] = shift(block, "chan", -TEAM * hop)
        return direct

    def gather(chunk, direct, after_far, after_pick, after_merge):
        edge = swap(far(direct[-hops], direct[hops], after_far), 2)
        crossed = [beside if hop == 0 else swap(direct[hop], 2) for hop in range(1 - hops, hops)]
        sources = [direct[hop] for hop in range(-hops, hops + 1)] + crossed + [edge]
        first, last = EDGES[chunk], EDGES[chunk + 1]
        keep, send = pick(hops, first, last - first, pair_offsets, core_offsets, sources, after_pick)
        chosen = merge(pair_offsets, keep, [swap(part, 1) for part in send], after_merge)
        return [chosen] + [shift(chosen, "win", step) for step in range(1, win)], send

    directs = [spread(block) for block in chunks]
    beside = swap(whole, 2)
    own = [row_parts[0]] + [shift(row_parts[step], "win", step) for step in range(1, win)]
    lags = [lay_out_lags(part) for part in own]

    pieces = []
    after_far, after_pick, after_merge = [core_offsets] + own[1:], [], []
    for chunk in range(CHUNKS):
        piece, send = gather(chunk, directs[chunk], after_far, after_pick, after_merge)
        after_far, after_pick, after_merge = [], [piece[0]] + lags[1:], piece[1:]
        pieces.append(piece)
    others = [[pieces[chunk][step] for chunk in range(CHUNKS)] for step in range(win)]
    acc = accumulate(None, lags[0], list(zip(EDGES, others[0])))
    left = [(step, chunk) for chunk in range(CHUNKS) for step in range(1, win)]
    for step, chunk in left[:-1]:
        acc = accumulate(acc, lags[step], [(EDGES[chunk], others[step][chunk])])
    step, chunk = left[-1]
    return finish(reach, factor, pair_offsets, acc, lags[step], EDGES[chunk], others[step][chunk])


def solution(mesh):
    placed = (P("chan", "win"), P(), P("chan", None))
    return jax.shard_map(
        body,
        mesh=mesh,
        in_specs=placed,
        out_specs=P(("chan", "win"), None, None, None),
        check_vma=False,
    )
```
